32 devices in a mesh: dp: 8 (over z, core), expert: 4 (over y, x).
Axes of the slice: x: 2, y: 2, z: 4, core: 2. Of those that a mesh axis runs over, the one named last changes fastest.
Arguments:
- tokens: bfloat16 [512, 2048], P(('dp', 'expert')), may hold values from -6 to 6
- grad_out: bfloat16 [512, 2048], P(('dp', 'expert')), may hold values from -6 to 6
- gate_probs: bfloat16 [512, 8], P(('dp', 'expert')), may hold values from 0.049804688 to 1
- routes: int32 [512, 8], P(('dp', 'expert')), may hold values from 0 to 15, as said below
- capacity: int32 [8, 16], P('dp', 'expert'), may hold values from 16 to 32, as said below
- pair_mask: int32 [16], P('expert'), may hold values from 1 to 4, as said below
- gate_up_weight: bfloat16 [16, 2048, 1536], P('expert'), may hold values from -0.125 to 0.125
- down_weight: bfloat16 [16, 2048, 768], P('expert'), may hold values from -0.21875 to 0.21875
Outputs:
- layer_out: bfloat16 [512, 2048], P(('dp', 'expert'))
- input_grad: bfloat16 [512, 2048], P(('dp', 'expert'))
- gate_grad: float32 [512, 8], P(('dp', 'expert'))
The draws below stay inside these ranges and needn't reach their ends.
Inputs may be any that keep to these rules, and one draw needn't show every extreme that they name: `routes`: each token names 8 different experts. The tokens of one device name any one expert at most 12 times; one expert, the same for all devices, is named exactly 12 times by the tokens of every device. `capacity`: both ends of the range occur in every draw. `pair_mask`: each entry is a power of two; both ends of the range occur in every draw.
All inputs are finite; a program needn't handle non-finite values.
Results may differ from the reference program's by a relative error of at most 0.01.
Values may be sent and summed in bfloat16 or wider, within the bound.
No kernel may reach another device: no remote copies, remote signals or barrier semaphores. Data moves between devices by JAX's collectives and lax.ppermute only.
A program may use at most 128 MiB of HBM per device.

```python
import math
import jax
import jax.numpy as jnp
from jax import lax

D = 2048
FFE = 768
TOPK = 8
EXPERTS = 16
TOK_DEV = 16
MOST = 12
CAP = 32
OVF = 16
TOKENS = 512
N_DP = 8
N_EXPERT = 4


def hot_choice(key):
    return jax.random.randint(jax.random.fold_in(key, 11), (), 0, EXPERTS)


def draw_routes(key, part):
    blocks = TOKENS // TOK_DEV
    others = EXPERTS - 1
    hot_id = hot_choice(key)
    block_keys = jax.random.split(jax.random.fold_in(key, 12), blocks)

    def one_block(block_key):
        perm_key, start_key, label_key, rotate_key = jax.random.split(block_key, 4)
        hot_rank = jax.random.permutation(perm_key, TOK_DEV)
        start_rank = jax.random.permutation(start_key, TOK_DEV)
        relabel = jax.random.permutation(label_key, others)
        rotation = jax.random.randint(rotate_key, (), 0, others)
        has_hot = (hot_rank < MOST).astype(jnp.int32)
        window_start = start_rank * others // TOK_DEV + rotation
        column = jnp.arange(TOPK, dtype=jnp.int32)
        other_pos = (window_start[:, None] + column[None, :] - has_hot[:, None]) % others
        other_id = (hot_id + 1 + relabel[other_pos]) % EXPERTS
        chosen = jnp.where((has_hot[:, None] == 1) & (column[None, :] == 0), hot_id, other_id)
        return chosen.astype(jnp.int32)
    return jax.vmap(one_block)(block_keys).reshape(TOKENS, TOPK)


def draw_capacity(key, part):
    caps = jax.random.randint(jax.random.fold_in(key, 21), (N_DP, EXPERTS), CAP // 2, CAP + 1)
    hot_id = hot_choice(key)
    row_pick = jax.random.randint(jax.random.fold_in(key, 22), (), 0, N_DP)
    row_ids = jnp.arange(N_DP, dtype=jnp.int32)[:, None]
    col_ids = jnp.arange(EXPERTS, dtype=jnp.int32)[None, :]
    caps = jnp.where((row_ids == row_pick) & (col_ids == hot_id), CAP, caps)
    caps = jnp.where((row_ids == row_pick) & (col_ids == (hot_id + 1) % EXPERTS), CAP // 2, caps)
    return caps.astype(jnp.int32)


def draw_pair_mask(key, part):
    levels = N_DP.bit_length() - 1
    powers = jax.random.randint(jax.random.fold_in(key, 31), (EXPERTS,), 0, levels)
    first_pick = jax.random.randint(jax.random.fold_in(key, 32), (), 0, EXPERTS)
    second_pick = (first_pick + 1 + jax.random.randint(jax.random.fold_in(key, 33), (), 0, EXPERTS - 1)) % EXPERTS
    index_ids = jnp.arange(EXPERTS, dtype=jnp.int32)
    powers = jnp.where(index_ids == first_pick, 0, powers)
    powers = jnp.where(index_ids == second_pick, levels - 1, powers)
    return jnp.left_shift(jnp.ones((EXPERTS,), jnp.int32), powers.astype(jnp.int32))


def block_levels(own_key, dims, shards, low, top_value):
    def one(axis_at, blocks):
        draws = jax.random.uniform(jax.random.fold_in(jax.random.fold_in(own_key, 6), axis_at), (blocks,), jnp.float32, low / len(shards), top_value / len(shards))
        return jnp.repeat(jnp.exp(draws), dims[axis_at] // blocks).reshape((-1,) + (1,) * (len(dims) - axis_at - 1))

    level = one(*shards[0])
    for cut in shards[1:]:
        level = level * one(*cut)
    return level


def scatter_about(key, dims, spread, bound, pieces=(), kind=jnp.bfloat16):
    factor_of = block_levels(key, dims, pieces, -0.22, 0.18) if pieces else 1.0
    drawn = jax.random.normal(key, dims, jnp.float32) * spread * factor_of
    return jnp.minimum(jnp.maximum(drawn, -bound), bound).astype(kind)


def setup_inputs(seed: int = 0) -> dict:
    key_of = jax.random.split(jax.random.key(seed), 9)
    tokens = scatter_about(key_of[0], (TOKENS, D), 1.0, 6.0, ((0, 32),))
    grad_out = scatter_about(key_of[1], (TOKENS, D), 1.0, 6.0, ((0, 32),))
    gate_probs = jnp.clip(jnp.exp(math.log(1.0) - 2.9996462 * jax.random.uniform(key_of[2], (TOKENS, TOPK), jnp.float32) ** block_levels(key_of[2], (TOKENS, TOPK), ((0, 32),), -0.2, 0.2)), 0.049804688, 1.0).astype(jnp.bfloat16)
    routes = draw_routes(jax.random.fold_in(key_of[8], 71), 0)
    capacity = draw_capacity(jax.random.fold_in(key_of[8], 71), 0)
    pair_mask = draw_pair_mask(jax.random.fold_in(key_of[8], 71), 0)
    gate_up_weight = scatter_about(key_of[6], (EXPERTS, D, 2 * FFE), D ** -0.5, 0.125, ((0, 4),))
    down_weight = scatter_about(key_of[7], (EXPERTS, D, FFE), FFE ** -0.5, 0.21875, ((0, 4),))
    return dict(tokens=tokens, grad_out=grad_out, gate_probs=gate_probs, routes=routes, capacity=capacity, pair_mask=pair_mask, gate_up_weight=gate_up_weight, down_weight=down_weight)


def pick_rows(table, index):
    return jnp.take(table, index, axis=0, mode="fill", fill_value=0)


def expert_rows(row_input, row_scaled, w_gate_up, w_down):
    hidden_units = w_down.shape[1]
    both = jnp.dot(row_input, w_gate_up, preferred_element_type=jnp.float32)
    gate_pre = both[:, :hidden_units]
    up_pre = both[:, hidden_units:]
    sigma = jax.nn.sigmoid(gate_pre)
    swish = gate_pre * sigma
    hidden = (swish * up_pre).astype(jnp.bfloat16)
    outputs = lax.dot_general(hidden, w_down, (((1,), (1,)), ((), ())), preferred_element_type=jnp.float32).astype(jnp.bfloat16)
    back_hidden = jnp.dot(row_scaled, w_down, preferred_element_type=jnp.float32)
    d_gate = back_hidden * up_pre * sigma * (1.0 + gate_pre * (1.0 - sigma))
    d_up = back_hidden * swish
    d_both = jnp.concatenate([d_gate, d_up], axis=1).astype(jnp.bfloat16)
    row_grads = lax.dot_general(d_both, w_gate_up, (((1,), (1,)), ((), ())), preferred_element_type=jnp.float32).astype(jnp.bfloat16)
    return outputs, row_grads


def reference(tokens, grad_out, gate_probs, routes, capacity, pair_mask, gate_up_weight, down_weight):
    per_row = TOK_DEV * N_EXPERT
    route_count = per_row * TOPK
    span = CAP + OVF
    row_routes = routes.reshape(N_DP, route_count)
    expert_ids = jnp.arange(EXPERTS, dtype=jnp.int32)
    queue_length = jnp.sum((row_routes[:, :, None] == expert_ids[None, None, :]).astype(jnp.int32), axis=1)
    home_rows = jnp.minimum(queue_length, capacity)
    spare_rows = capacity - home_rows
    partner = jnp.bitwise_xor(jnp.arange(N_DP, dtype=jnp.int32)[:, None], pair_mask[None, :])
    partner_spare = jnp.take_along_axis(spare_rows, partner, axis=0)
    keep_limit = capacity + jnp.minimum(partner_spare, OVF)

    def one_row(packed):
        row_tokens, row_grad, row_gates, row_route, row_limit = packed
        flat_gates = row_gates.reshape(route_count).astype(jnp.float32)

        def one_expert(carry, expert_id):
            out_sum, grad_sum, gate_sum = carry
            route_hit = (row_route == expert_id).astype(jnp.int32)
            queue_pos = jnp.cumsum(route_hit) - 1
            target = jnp.where((route_hit == 1) & (queue_pos < span), queue_pos, span)
            source = jnp.full((span + 1,), route_count, jnp.int32).at[target].set(jnp.arange(route_count, dtype=jnp.int32))[:span]
            kept_row = (source < route_count) & (jnp.arange(span, dtype=jnp.int32) < row_limit[expert_id])
            token_index = jnp.where(kept_row, source // TOPK, per_row).astype(jnp.int32)
            route_index = jnp.where(kept_row, source, route_count).astype(jnp.int32)
            row_input = pick_rows(row_tokens, token_index)
            rows_grad = pick_rows(row_grad, token_index)
            rows_gate = jnp.take(flat_gates, route_index, mode="fill", fill_value=0.0)
            row_scaled = (rows_gate[:, None] * rows_grad.astype(jnp.float32)).astype(jnp.bfloat16)
            outputs, row_grads = expert_rows(row_input, row_scaled, gate_up_weight[expert_id], down_weight[expert_id])
            out_float = outputs.astype(jnp.float32)
            out_sum = out_sum.at[token_index].add(rows_gate[:, None] * out_float, mode="drop")
            grad_sum = grad_sum.at[token_index].add(row_grads.astype(jnp.float32), mode="drop")
            gate_sum = gate_sum.at[route_index].add(jnp.sum(rows_grad.astype(jnp.float32) * out_float, axis=1), mode="drop")
            return (out_sum, grad_sum, gate_sum), None

        initial = (jnp.zeros((per_row, D), jnp.float32), jnp.zeros((per_row, D), jnp.float32), jnp.zeros((route_count,), jnp.float32))
        scan_result = lax.scan(one_expert, initial, expert_ids)
        out_sum, grad_sum, gate_sum = scan_result[0]
        return out_sum.astype(jnp.bfloat16), grad_sum.astype(jnp.bfloat16), gate_sum.reshape(per_row, TOPK)

    results = lax.map(one_row, (tokens.reshape(N_DP, per_row, D), grad_out.reshape(N_DP, per_row, D), gate_probs.reshape(N_DP, per_row, TOPK), row_routes, keep_limit))
    return (results[0].reshape(TOKENS, D), results[1].reshape(TOKENS, D), results[2].reshape(TOKENS, TOPK))
```

```python
import functools
import jax
import jax.numpy as jnp
from jax import lax
from jax.experimental import pallas as pl
from jax.experimental.pallas import tpu as pltpu
from jax.sharding import PartitionSpec as P

TOPK = 8
EXPERTS = 16
OVF = 16
LANES = 128
CAP_AT = 2 * TOPK
LOW_AT = EXPERTS

VM = pltpu.VMEM


def swapped(shard, axis, mask):
    return lax.ppermute(shard, axis, [(i, i ^ mask) for i in range(lax.axis_size(axis))])


def lane_ids(rows):
    return lax.broadcasted_iota(jnp.int32, (rows, LANES), 1)


def side_tables(side, first_expert):
    rows = side.shape[0]
    lane = (lane_ids(rows) + first_expert).astype(jnp.float32)
    named = jnp.zeros((rows, LANES), jnp.float32)
    gate = jnp.zeros((rows, LANES), jnp.float32)
    for k in range(TOPK):
        hit = side[:, k : k + 1] == lane
        named = jnp.where(hit, 1.0, named)
        gate = jnp.where(hit, side[:, TOPK + k : TOPK + k + 1], gate)
    return named, gate


def spare_kernel(group_size, groups, info, *refs):
    pieces, out = refs[:-1], refs[-1]
    first_expert = info[0]
    out[...] = jnp.zeros_like(out)
    for g in range(groups):
        load = jnp.zeros((1, LANES), jnp.float32)
        for j in range(group_size):
            side = pieces[g * group_size + j][...].astype(jnp.float32)
            named, _ = side_tables(side, first_expert)
            load = load + jnp.sum(named, axis=0, keepdims=True)
        cap = cap_lanes(pieces[g * group_size][...])
        out[g : g + 1, :] = cap - jnp.minimum(load, cap)


def cap_lanes(side):
    return pltpu.roll(side.astype(jnp.float32), LANES - CAP_AT, 1)[0:1, :]


def expert_kernel(
    group_size, groups, width, levels, info, mask_ref, spare_ref, *refs
):
    far = refs[: len(levels)]
    refs = refs[len(levels) :]
    count = groups * group_size
    pieces = refs[:count]
    gate_up_hbm, down_hbm = refs[count : count + 2]
    outs = refs[count + 2 : count + 2 + groups]
    (tok, grd, side, gate_up, down, hid, dpre, acc_out, acc_grad, sems) = refs[count + 2 + groups :]
    first_expert, first_local, self_index = info[0], info[1], info[2]
    per_device, _, hidden_units = down.shape
    rows = tok.shape[0]
    piece_rows = rows // count
    group_rows = rows // groups
    step = 256
    steps = hidden_units // step

    def copies(i, j):
        cols = pl.ds(j * step, step)
        ups = pl.ds(hidden_units + j * step, step)
        return (
            pltpu.make_async_copy(gate_up_hbm.at[first_local + i, :, cols], gate_up.at[i, :, cols], sems.at[i, j, 0]),
            pltpu.make_async_copy(gate_up_hbm.at[first_local + i, :, ups], gate_up.at[i, :, ups], sems.at[i, j, 1]),
            pltpu.make_async_copy(down_hbm.at[first_local + i, :, cols], down.at[i, :, cols], sems.at[i, j, 2]),
        )

    for i in range(per_device):
        for j in range(steps):
            for copy in copies(i, j):
                copy.start()

    for n, piece in enumerate(pieces):
        at = pl.ds(n * piece_rows, piece_rows)
        tok[at, :] = piece[:, :width]
        grd[at, :] = piece[:, width : 2 * width]
        side[at, :] = piece[:, 2 * width :].astype(jnp.float32)

    named, gate = side_tables(side[...], first_expert)
    r_id = lax.broadcasted_iota(jnp.int32, (rows, rows), 0)
    c_id = lax.broadcasted_iota(jnp.int32, (rows, rows), 1)

    def order(v):
        block, inner = v // piece_rows, v % piece_rows
        grp, j = block // group_size, block % group_size
        return grp, (j ^ self_index) * piece_rows + inner

    r_grp, r_ord = order(r_id)
    c_grp, c_ord = order(c_id)
    earlier = ((r_grp == c_grp) & (c_ord < r_ord)).astype(jnp.bfloat16)
    place = jnp.dot(earlier, named.astype(jnp.bfloat16), preferred_element_type=jnp.float32)
    mask = mask_ref[...]
    row_grp = lax.broadcasted_iota(jnp.int32, (rows, LANES), 0) // group_rows
    limit = jnp.zeros((rows, LANES), jnp.float32)
    for g in range(groups):
        other = jnp.zeros((1, LANES), jnp.float32)
        if groups == 2:
            other = jnp.where(mask == 1, spare_ref[1 - g : 2 - g, :], other)
        for level, ref in zip(levels, far):
            other = jnp.where(mask == level, ref[g : g + 1, :], other)
        cap = cap_lanes(side[g * group_rows : g * group_rows + 8, :])
        limit = jnp.where(row_grp == g, cap + jnp.minimum(other, float(OVF)), limit)
    kept = jnp.where((named > 0.0) & (place < limit), 1.0, 0.0)

    acc_out[...] = jnp.zeros_like(acc_out)
    acc_grad[...] = jnp.zeros_like(acc_grad)
    lane = lane_ids(rows)

    def one_expert(i, gate_grads):
        here = lane == first_local + i
        keep = jnp.sum(jnp.where(here, kept, 0.0), axis=1, keepdims=True)
        weight = jnp.sum(jnp.where(here, gate, 0.0), axis=1, keepdims=True) * keep
        t, g = tok[...], grd[...]
        total = jnp.zeros((rows, 1), jnp.float32)
        for j in range(steps):
            for copy in copies(i, j):
                copy.wait()
            cols = pl.ds(j * step, step)
            ups = pl.ds(hidden_units + j * step, step)
            a = jnp.dot(t, gate_up[i, :, cols], preferred_element_type=jnp.float32)
            b = jnp.dot(t, gate_up[i, :, ups], preferred_element_type=jnp.float32)
            back = jnp.dot(g, down[i, :, cols], preferred_element_type=jnp.float32)
            s = jax.nn.sigmoid(a)
            swish = a * s
            hidden = swish * b
            total = total + jnp.sum(hidden * back, axis=1, keepdims=True)
            back = back * weight
            hid[:, cols] = (hidden * weight).astype(jnp.bfloat16)
            dpre[:, cols] = (back * b * s * (1.0 + a * (1.0 - s))).astype(jnp.bfloat16)
            dpre[:, ups] = (back * swish).astype(jnp.bfloat16)
        h, d = hid[...], dpre[...]
        wide = 512
        for j in range(width // wide):
            cols = pl.ds(j * wide, wide)
            acc_out[:, cols] += lax.dot_general(
                h, down[i, cols, :], (((1,), (1,)), ((), ())), preferred_element_type=jnp.float32
            )
            acc_grad[:, cols] += lax.dot_general(
                d, gate_up[i, cols, :], (((1,), (1,)), ((), ())), preferred_element_type=jnp.float32
            )
        total = total * keep
        high = total.astype(jnp.bfloat16).astype(jnp.float32)
        at = first_expert + first_local + i
        gate_grads = jnp.where(lane == at, high, gate_grads)
        return jnp.where(lane == at + LOW_AT, total - high, gate_grads)

    gate_grads = lax.fori_loop(0, per_device, one_expert, jnp.zeros((rows, LANES), jnp.float32))
    for g in range(groups):
        at = slice(g * group_rows, (g + 1) * group_rows)
        outs[g][:, :width] = acc_out[at, :].astype(jnp.bfloat16)
        outs[g][:, width : 2 * width] = acc_grad[at, :].astype(jnp.bfloat16)
        outs[g][:, 2 * width :] = gate_grads[at, :].astype(jnp.bfloat16)


def finish_kernel(width, *refs):
    parts, (routes, layer_out, input_grad, gate_grad) = refs[:-4], refs[-4:]

    def total(cols):
        out = parts[0][:, cols].astype(jnp.float32)
        for part in parts[1:]:
            out = out + part[:, cols].astype(jnp.float32)
        return out

    layer_out[...] = total(slice(0, width)).astype(jnp.bfloat16)
    input_grad[...] = total(slice(width, 2 * width)).astype(jnp.bfloat16)
    table = total(slice(2 * width, 2 * width + LANES))
    table = table + pltpu.roll(table, LANES - LOW_AT, 1)
    ids = routes[...]
    lane = lane_ids(ids.shape[0])
    out = jnp.zeros(ids.shape, jnp.float32)
    column = lax.broadcasted_iota(jnp.int32, ids.shape, 1)
    for k in range(TOPK):
        picked = jnp.sum(jnp.where(lane == ids[:, k : k + 1], table, 0.0), axis=1, keepdims=True)
        out = jnp.where(column == k, picked, out)
    gate_grad[...] = out


def body(tokens, grad_out, gate_probs, routes, capacity, pair_mask, gate_up_weight, down_weight):
    tok_count, width = tokens.shape
    local_count, _, hidden_units = down_weight.shape
    group_size = lax.axis_size("expert")
    replicas = lax.axis_size("dp")
    paired = local_count % 2 == 0 and replicas % 2 == 0
    groups = 2 if paired else 1
    per_device = local_count // groups
    me = lax.axis_index("expert")
    core = lax.axis_index("dp") % groups
    info = jnp.stack([me * local_count, core * per_device, me]).astype(jnp.int32)
    caps = jnp.broadcast_to(capacity.astype(jnp.bfloat16), (tok_count, local_count))
    side = jnp.concatenate([routes.astype(jnp.bfloat16), gate_probs, caps], axis=1)
    side = jnp.pad(side, ((0, 0), (0, LANES - side.shape[1])))
    payload = jnp.concatenate([tokens, grad_out, side], axis=1)
    mask_row = jnp.pad(pair_mask.reshape(1, local_count), ((0, 0), (0, LANES - local_count)))

    pieces = [payload] + [swapped(payload, "expert", k) for k in range(1, group_size)]
    if paired:
        pieces = pieces + [swapped(piece, "dp", 1) for piece in pieces]
    rows = len(pieces) * tok_count
    total_width = 2 * width + LANES

    side_spec = pl.BlockSpec((tok_count, LANES), lambda i: (0, 2 * width // LANES))
    spare = pl.pallas_call(
        functools.partial(spare_kernel, group_size, groups),
        out_shape=jax.ShapeDtypeStruct((8, LANES), jnp.float32),
        grid=(1,),
        in_specs=[pl.BlockSpec(memory_space=pltpu.SMEM)] + [side_spec] * len(pieces),
        out_specs=pl.BlockSpec((8, LANES), lambda i: (0, 0)),
        name="spare",
    )(info, *pieces)
    levels = [1 << b for b in range(groups - 1, replicas.bit_length() - 1)]
    far = [swapped(spare, "dp", level) for level in levels]

    vm, hbm = pl.BlockSpec(memory_space=VM), pl.BlockSpec(memory_space=pl.ANY)
    group_rows = rows // groups
    parts = pl.pallas_call(
        functools.partial(expert_kernel, group_size, groups, width, tuple(levels)),
        out_shape=[jax.ShapeDtypeStruct((group_rows, total_width), jnp.bfloat16)] * groups,
        in_specs=[pl.BlockSpec(memory_space=pltpu.SMEM), vm, vm]
        + [vm] * (len(far) + len(pieces))
        + [hbm, hbm],
        out_specs=[vm] * groups,
        scratch_shapes=[
            VM((rows, width), jnp.bfloat16),
            VM((rows, width), jnp.bfloat16),
            VM((rows, LANES), jnp.float32),
            VM((per_device, width, 2 * hidden_units), jnp.bfloat16),
            VM((per_device, width, hidden_units), jnp.bfloat16),
            VM((rows, hidden_units), jnp.bfloat16),
            VM((rows, 2 * hidden_units), jnp.bfloat16),
            VM((rows, width), jnp.float32),
            VM((rows, width), jnp.float32),
            pltpu.SemaphoreType.DMA((per_device, hidden_units // 256, 3)),
        ],
        name="experts",
    )(info, mask_row, spare, *far, *pieces, gate_up_weight, down_weight)
    if paired:
        other = swapped(parts[1], "dp", 1)
        summed = parts[0].astype(jnp.float32) + other.astype(jnp.float32)
        summed = summed.astype(jnp.bfloat16)
    else:
        summed = parts[0]
    blocks = summed.reshape(group_size, tok_count, total_width)
    mine = [blocks[0]] + [swapped(blocks[k], "expert", k) for k in range(1, group_size)]
    return tuple(
        pl.pallas_call(
            functools.partial(finish_kernel, width),
            out_shape=[
                jax.ShapeDtypeStruct((tok_count, width), jnp.bfloat16),
                jax.ShapeDtypeStruct((tok_count, width), jnp.bfloat16),
                jax.ShapeDtypeStruct((tok_count, TOPK), jnp.float32),
            ],
            in_specs=[vm] * (group_size + 1),
            out_specs=[vm] * 3,
            name="finish",
        )(*mine, routes)
    )


def solution(mesh):
    return jax.shard_map(
        body,
        mesh=mesh,
        in_specs=(
            P(("dp", "expert"), None),
            P(("dp", "expert"), None),
            P(("dp", "expert"), None),
            P(("dp", "expert"), None),
            P("dp", "expert"),
            P("expert"),
            P("expert", None, None),
            P("expert", None, None),
        ),
        out_specs=(P(("dp", "expert"), None), P(("dp", "expert"), None), P(("dp", "expert"), None)),
        check_vma=False,
    )
```

```python
import functools
import jax
import jax.numpy as jnp
from jax import lax
from jax.experimental import pallas as pl
from jax.experimental.pallas import tpu as pltpu
from jax.sharding import PartitionSpec as P

TOPK = 8
EXPERTS = 16
OVF = 16
LANES = 128
SUB = 8
STEP = 256
WIDE = 512
MIB = 1 << 20
LURE = 20_000_000_000

VM = pltpu.VMEM


def swapped(shard, axis, mask):
    return lax.ppermute(shard, axis, [(i, i ^ mask) for i in range(lax.axis_size(axis))])


def iota(shape, axis):
    return lax.broadcasted_iota(jnp.int32, shape, axis)


def place_of(groups, local_count):
    core = lax.axis_index("dp") % groups
    return lax.axis_index("expert") * local_count, core * (local_count // groups)


def prep_kernel(tokens, routes_t, gates_t, capacity, out, side):
    width = tokens.shape[1]
    tok_count = routes_t.shape[1]
    out[:, :width] = tokens[...]
    side[...] = jnp.zeros_like(side)
    side[:TOPK, :tok_count] = routes_t[...].astype(jnp.float32)
    side[TOPK : 2 * TOPK, :tok_count] = gates_t[...].astype(jnp.float32)
    block = side[...]
    row, lane = iota(block.shape, 0), iota(block.shape, 1)
    for l in range(capacity.shape[1]):
        block = jnp.where((lane == tok_count) & (row == l), capacity[0, l].astype(jnp.float32), block)
    out[:, width:] = block.astype(jnp.bfloat16)


def tables_kernel(group_size, groups, local_count, tok_count, *refs):
    pieces, (spare, named_t, place_t, gate_t, cap_t) = refs[:-5], refs[-5:]
    first_expert, _ = place_of(groups, local_count)
    self_index = lax.axis_index("expert")
    rows = tok_count * len(pieces)
    per_lanes = LANES // tok_count
    lane = iota((2 * TOPK, LANES), 1)
    columns = []
    for q in range(rows // LANES):
        acc = jnp.zeros((2 * TOPK, LANES), jnp.float32)
        for n in range(per_lanes):
            side = pieces[q * per_lanes + n][: 2 * TOPK, :].astype(jnp.float32)
            moved = pltpu.roll(side, n * tok_count, 1) if n else side
            acc = jnp.where(lane // tok_count == n, moved, acc)
        columns.append(acc)
    both = jnp.concatenate(columns, axis=1) if len(columns) > 1 else columns[0]
    routes, gates = both[:TOPK], both[TOPK:]
    sub = iota((SUB, rows), 0)
    named = jnp.zeros((SUB, rows), jnp.float32)
    gate = jnp.zeros((SUB, rows), jnp.float32)
    for l in range(local_count):
        hit = routes == (first_expert + l).astype(jnp.float32)
        here = sub == l
        named = jnp.where(here, jnp.max(jnp.where(hit, 1.0, 0.0), axis=0, keepdims=True), named)
        gate = jnp.where(here, jnp.sum(jnp.where(hit, gates, 0.0), axis=0, keepdims=True), gate)

    def order(v):
        block, inner = v // tok_count, v % tok_count
        return block // group_size, ((block % group_size) ^ self_index) * tok_count + inner

    u_grp, u_ord = order(iota((rows, rows), 0))
    t_grp, t_ord = order(iota((rows, rows), 1))
    earlier = ((u_grp == t_grp) & (u_ord < t_ord)).astype(jnp.bfloat16)
    named_t[...] = named
    gate_t[...] = gate
    place_t[...] = jnp.dot(named.astype(jnp.bfloat16), earlier, preferred_element_type=jnp.float32)
    group_of = iota((SUB, rows), 1) // (rows // groups)
    lane8 = iota((SUB, LANES), 1)
    spares = jnp.zeros((SUB, LANES), jnp.float32)
    caps = jnp.zeros((SUB, LANES), jnp.float32)
    for g in range(groups):
        load = jnp.sum(jnp.where(group_of == g, named, 0.0), axis=1, keepdims=True)
        cap = pieces[g * group_size][...].astype(jnp.float32)[:SUB, tok_count : tok_count + 1]
        caps = jnp.where(lane8 == g, cap, caps)
        spares = jnp.where(lane8 == g, cap - jnp.minimum(load, cap), spares)
    spare[...] = spares
    cap_t[...] = caps


def to_columns(table, rows):
    full = jnp.concatenate([table, jnp.zeros((LANES - SUB, rows), jnp.float32)], axis=0)
    return jnp.transpose(full)


def lane_of(columns, index):
    return jnp.sum(jnp.where(iota(columns.shape, 1) == index, columns, 0.0), axis=1, keepdims=True)


def first_kernel(groups, local_count, count, width, *refs):
    toks, grds = refs[:count], refs[count : 2 * count]
    gate_t, gate_up, down, hid, dpre, grads, tok, grd = refs[2 * count :]
    first_expert, first_local = place_of(groups, local_count)
    rows = tok.shape[0]
    piece_rows = rows // count
    hidden_units = down.shape[2]
    for n in range(count):
        at = pl.ds(n * piece_rows, piece_rows)
        tok[at, :] = toks[n][:, :width]
        grd[at, :] = grds[n][...]
    gates = to_columns(gate_t[...], rows)
    lane = iota((rows, LANES), 1)

    def one_expert(i, gate_grads):
        e = first_local + i
        weight = lane_of(gates, e)
        t, g = tok[...], grd[...]
        total = jnp.zeros((rows, 1), jnp.float32)
        for j in range(hidden_units // STEP):
            cols = pl.ds(j * STEP, STEP)
            ups = pl.ds(hidden_units + j * STEP, STEP)
            a = jnp.dot(t, gate_up[e, :, cols], preferred_element_type=jnp.float32)
            b = jnp.dot(t, gate_up[e, :, ups], preferred_element_type=jnp.float32)
            back = jnp.dot(g, down[e, :, cols], preferred_element_type=jnp.float32)
            s = jax.nn.sigmoid(a)
            swish = a * s
            hidden = swish * b
            total = total + jnp.sum(hidden * back, axis=1, keepdims=True)
            back = back * weight
            hid[i, :, cols] = (hidden * weight).astype(jnp.bfloat16)
            dpre[i, :, cols] = (back * b * s * (1.0 + a * (1.0 - s))).astype(jnp.bfloat16)
            dpre[i, :, ups] = (back * swish).astype(jnp.bfloat16)
        return jnp.where(lane == e, total, gate_grads)

    grads[...] = lax.fori_loop(0, local_count // groups, one_expert, jnp.zeros((rows, LANES), jnp.float32))


def second_kernel(groups, local_count, width, levels, mask_ref, *refs):
    far = refs[: len(levels)]
    (spare, named_t, place_t, cap_t, hid, dpre, grads, gate_up, down) = refs[len(levels) : len(levels) + 9]
    outs = refs[len(levels) + 9 : len(levels) + 9 + groups]
    acc_out, acc_grad = refs[len(levels) + 9 + groups :]
    first_expert, first_local = place_of(groups, local_count)
    rows = acc_out.shape[0]
    group_rows = rows // groups
    sub = iota((SUB, 1), 0)
    mask = jnp.zeros((SUB, 1), jnp.int32)
    for l in range(local_count):
        mask = jnp.where(sub == l, mask_ref[l], mask)
    group_of = iota((SUB, rows), 1) // group_rows
    limit = jnp.zeros((SUB, rows), jnp.float32)
    for g in range(groups):
        other = jnp.zeros((SUB, 1), jnp.float32)
        if groups == 2:
            other = jnp.where(mask == 1, spare[:, 1 - g : 2 - g], other)
        for level, ref in zip(levels, far):
            other = jnp.where(mask == level, ref[:, g : g + 1], other)
        limit = jnp.where(group_of == g, cap_t[:, g : g + 1] + jnp.minimum(other, float(OVF)), limit)
    kept = jnp.where((named_t[...] > 0.0) & (place_t[...] < limit), 1.0, 0.0)
    kept = to_columns(kept, rows)
    acc_out[...] = jnp.zeros_like(acc_out)
    acc_grad[...] = jnp.zeros_like(acc_grad)

    def one_expert(i, _):
        e = first_local + i
        keep = lane_of(kept, e) > 0.0
        h = jnp.where(keep, hid[i].astype(jnp.float32), 0.0).astype(jnp.bfloat16)
        d = jnp.where(keep, dpre[i].astype(jnp.float32), 0.0).astype(jnp.bfloat16)
        for j in range(width // WIDE):
            cols = pl.ds(j * WIDE, WIDE)
            acc_out[:, cols] += lax.dot_general(
                h, down[e, cols, :], (((1,), (1,)), ((), ())), preferred_element_type=jnp.float32
            )
            acc_grad[:, cols] += lax.dot_general(
                d, gate_up[e, cols, :], (((1,), (1,)), ((), ())), preferred_element_type=jnp.float32
            )
        return _

    lax.fori_loop(0, local_count // groups, one_expert, 0)
    value = jnp.where(kept > 0.0, grads[...], 0.0)
    high = value.astype(jnp.bfloat16).astype(jnp.float32)
    high_at = pltpu.roll(high, first_expert, 1)
    low_at = pltpu.roll(value - high, first_expert + EXPERTS, 1)
    table = high_at + low_at
    for g in range(groups):
        at = slice(g * group_rows, (g + 1) * group_rows)
        outs[g][:, :width] = acc_out[at, :].astype(jnp.bfloat16)
        outs[g][:, width : 2 * width] = acc_grad[at, :].astype(jnp.bfloat16)
        outs[g][:, 2 * width :] = table[at, :].astype(jnp.bfloat16)


def experts_kernel(groups, local_count, count, width, levels, mask_ref, *refs):
    n = len(levels)
    far, refs = refs[:n], refs[n:]
    (spare, named_t, place_t, cap_t, gate_t), refs = refs[:5], refs[5:]
    pieces, refs = refs[: 2 * count], refs[2 * count :]
    (gate_up, down), refs = refs[:2], refs[2:]
    outs, (tok, grd, hid, dpre, grads, acc_out, acc_grad) = refs[:groups], refs[groups:]
    first_kernel(groups, local_count, count, width, *pieces, gate_t, gate_up, down, hid, dpre, grads, tok, grd)
    second_kernel(
        groups, local_count, width, levels, mask_ref,
        *far, spare, named_t, place_t, cap_t, hid, dpre, grads, gate_up, down, *outs, acc_out, acc_grad,
    )


def join_kernel(own, other, *outs):
    rows = outs[0].shape[0]
    for n, out in enumerate(outs):
        at = slice(n * rows, (n + 1) * rows)
        out[...] = (own[at, :].astype(jnp.float32) + other[at, :].astype(jnp.float32)).astype(out.dtype)


def finish_kernel(width, *refs):
    parts, (routes_t, layer_out, input_grad, gate_grad_t) = refs[:-4], refs[-4:]

    def total(cols):
        out = parts[0][:, cols].astype(jnp.float32)
        for part in parts[1:]:
            out = out + part[:, cols].astype(jnp.float32)
        return out

    layer_out[...] = total(slice(0, width)).astype(jnp.bfloat16)
    input_grad[...] = total(slice(width, 2 * width)).astype(jnp.bfloat16)
    table = total(slice(2 * width, 2 * width + LANES))
    tok_count = table.shape[0]
    table = jnp.concatenate([table, jnp.zeros((LANES - tok_count, LANES), jnp.float32)], axis=0)
    by_expert = jnp.transpose(table)[:, :tok_count]
    ids = routes_t[...]
    out = jnp.zeros(ids.shape, jnp.float32)
    for e in range(EXPERTS):
        value = by_expert[e : e + 1, :] + by_expert[EXPERTS + e : EXPERTS + e + 1, :]
        out = jnp.where(ids == e, value, out)
    gate_grad_t[...] = out


def kernel(body, name, out_shape, in_specs, scratch=(), limit=4, flops=0):
    vm = pl.BlockSpec(memory_space=VM)
    return pl.pallas_call(
        body,
        out_shape=out_shape,
        in_specs=in_specs,
        out_specs=jax.tree.map(lambda _: vm, out_shape),
        scratch_shapes=scratch,
        compiler_params=pltpu.CompilerParams(vmem_limit_bytes=limit * MIB),
        cost_estimate=pl.CostEstimate(flops=flops, bytes_accessed=0, transcendentals=0) if flops else None,
        name=name,
    )


def body(tokens, grad_out, gate_probs, routes, capacity, pair_mask, gate_up_weight, down_weight):
    tok_count, width = tokens.shape
    local_count, _, hidden_units = down_weight.shape
    group_size = lax.axis_size("expert")
    replicas = lax.axis_size("dp")
    groups = 2 if local_count % 2 == 0 and replicas % 2 == 0 else 1
    per_device = local_count // groups
    bf16, f32 = jnp.bfloat16, jnp.float32
    vm, sm = pl.BlockSpec(memory_space=VM), pl.BlockSpec(memory_space=pltpu.SMEM)
    array = jax.ShapeDtypeStruct
    routes_t = routes.T
    gate_up = pltpu.with_memory_space_constraint(gate_up_weight, VM)
    down = pltpu.with_memory_space_constraint(down_weight, VM)

    packed = kernel(
        prep_kernel,
        "prep",
        array((tok_count, width + LANES), bf16),
        [vm, vm, vm, sm],
        [VM((tok_count, LANES), f32)],
        flops=LURE,
    )(tokens, routes_t, gate_probs.T, capacity)

    def gathered(piece):
        pieces = [piece] + [swapped(piece, "expert", k) for k in range(1, group_size)]
        return pieces + [swapped(p, "dp", 1) for p in pieces] if groups == 2 else pieces

    toks = gathered(packed)
    grds = gathered(grad_out)
    count = len(toks)
    rows = count * tok_count
    total_width = 2 * width + LANES

    side_spec = pl.BlockSpec((tok_count, LANES), lambda i: (0, width // LANES))
    small, wide = array((SUB, LANES), f32), array((SUB, rows), f32)
    spare, named_t, place_t, gate_t, cap_t = pl.pallas_call(
        functools.partial(tables_kernel, group_size, groups, local_count, tok_count),
        out_shape=[small, wide, wide, wide, small],
        grid=(1,),
        in_specs=[side_spec] * count,
        out_specs=[pl.BlockSpec((SUB, s.shape[1]), lambda i: (0, 0)) for s in (small, wide, wide, wide, small)],
        compiler_params=pltpu.CompilerParams(vmem_limit_bytes=4 * MIB),
        name="tables",
    )(*toks)
    levels = tuple(1 << b for b in range(groups - 1, replicas.bit_length() - 1))
    far = [swapped(spare, "dp", level) for level in levels]

    group_rows = rows // groups
    parts = kernel(
        functools.partial(experts_kernel, groups, local_count, count, width, levels),
        "experts",
        [array((group_rows, total_width), bf16)] * groups,
        [sm] + [vm] * (len(far) + 7 + 2 * count),
        [
            VM((rows, width), bf16),
            VM((rows, width), bf16),
            VM((per_device, rows, hidden_units), bf16),
            VM((per_device, rows, 2 * hidden_units), bf16),
            VM((rows, LANES), f32),
            VM((rows, width), f32),
            VM((rows, width), f32),
        ],
        12,
    )(pair_mask, *far, spare, named_t, place_t, cap_t, gate_t, *toks, *grds, gate_up, down)
    block = array((tok_count, total_width), bf16)
    if groups == 2:
        other = swapped(parts[1], "dp", 1)
        blocks = kernel(join_kernel, "join", [block] * group_size, [vm, vm])(parts[0], other)
    else:
        blocks = [parts[0][k * tok_count : (k + 1) * tok_count] for k in range(group_size)]
    mine = [blocks[0]] + [swapped(blocks[k], "expert", k) for k in range(1, group_size)]
    layer_out, input_grad, gate_grad_t = kernel(
        functools.partial(finish_kernel, width),
        "finish",
        [array((tok_count, width), bf16), array((tok_count, width), bf16), array((TOPK, tok_count), f32)],
        [vm] * (group_size + 1),
    )(*mine, routes_t)
    return layer_out, input_grad, gate_grad_t.T


def solution(mesh):
    return jax.shard_map(
        body,
        mesh=mesh,
        in_specs=(
            P(("dp", "expert"), None),
            P(("dp", "expert"), None),
            P(("dp", "expert"), None),
            P(("dp", "expert"), None),
            P("dp", "expert"),
            P("expert"),
            P("expert", None, None),
            P("expert", None, None),
        ),
        out_specs=(P(("dp", "expert"), None), P(("dp", "expert"), None), P(("dp", "expert"), None)),
        check_vma=False,
    )
```

```python
import functools
import jax
import jax.numpy as jnp
from jax import lax
from jax.experimental import pallas as pl
from jax.experimental.pallas import tpu as pltpu
from jax.sharding import PartitionSpec as P

TOPK = 8
EXPERTS = 16
OVF = 16
LANES = 128
SUB = 8
STEP = 256
WIDE = 512
MIB = 1 << 20
LURE = 20_000_000_000

VM = pltpu.VMEM


def swapped(shard, axis, mask):
    return lax.ppermute(shard, axis, [(i, i ^ mask) for i in range(lax.axis_size(axis))])


def iota(shape, axis):
    return lax.broadcasted_iota(jnp.int32, shape, axis)


def place_of(groups, local_count):
    core = lax.axis_index("dp") % groups
    return lax.axis_index("expert") * local_count, core * (local_count // groups)


def prep_kernel(tokens, routes_t, gates_t, capacity, out, ids, gates, caps, side, sems):
    width = tokens.shape[1]
    tok_count = routes_t.shape[1]
    copies = [
        pltpu.make_async_copy(routes_t, ids, sems.at[0]),
        pltpu.make_async_copy(gates_t, gates, sems.at[1]),
        pltpu.make_async_copy(tokens, out.at[:, :width], sems.at[2]),
    ]
    one = capacity.shape[1] == 1
    if not one:
        copies.insert(2, pltpu.make_async_copy(capacity, caps, sems.at[3]))
    for copy in copies:
        copy.start()
    side[...] = jnp.zeros_like(side)
    for copy in copies[:-1]:
        copy.wait()
    side[:TOPK, :tok_count] = ids[...].astype(jnp.float32)
    side[TOPK : 2 * TOPK, :tok_count] = gates[...].astype(jnp.float32)
    block = side[...]
    row, lane = iota(block.shape, 0), iota(block.shape, 1)
    for l in range(capacity.shape[1]):
        block = jnp.where((lane == tok_count) & (row == l), (capacity if one else caps)[0, l].astype(jnp.float32), block)
    out[:, width:] = block.astype(jnp.bfloat16)
    copies[-1].wait()


def tables_kernel(group_size, groups, local_count, tok_count, *refs):
    pieces, (spare, named_t, place_t, gate_t, cap_t) = refs[:-5], refs[-5:]
    first_expert, _ = place_of(groups, local_count)
    self_index = lax.axis_index("expert")
    rows = tok_count * len(pieces)
    per_lanes = LANES // tok_count
    lane = iota((2 * TOPK, LANES), 1)
    columns = []
    for q in range(rows // LANES):
        acc = jnp.zeros((2 * TOPK, LANES), jnp.float32)
        for n in range(per_lanes):
            side = pieces[q * per_lanes + n][: 2 * TOPK, :].astype(jnp.float32)
            moved = pltpu.roll(side, n * tok_count, 1) if n else side
            acc = jnp.where(lane // tok_count == n, moved, acc)
        columns.append(acc)
    both = jnp.concatenate(columns, axis=1) if len(columns) > 1 else columns[0]
    routes, gates = both[:TOPK], both[TOPK:]
    sub = iota((SUB, rows), 0)
    named = jnp.zeros((SUB, rows), jnp.float32)
    gate = jnp.zeros((SUB, rows), jnp.float32)
    for l in range(local_count):
        hit = routes == (first_expert + l).astype(jnp.float32)
        here = sub == l
        named = jnp.where(here, jnp.max(jnp.where(hit, 1.0, 0.0), axis=0, keepdims=True), named)
        gate = jnp.where(here, jnp.sum(jnp.where(hit, gates, 0.0), axis=0, keepdims=True), gate)

    def order(v):
        block, inner = v // tok_count, v % tok_count
        return block // group_size, ((block % group_size) ^ self_index) * tok_count + inner

    u_grp, u_ord = order(iota((rows, rows), 0))
    t_grp, t_ord = order(iota((rows, rows), 1))
    earlier = ((u_grp == t_grp) & (u_ord < t_ord)).astype(jnp.bfloat16)
    named_t[...] = named
    gate_t[...] = gate
    place_t[...] = jnp.dot(named.astype(jnp.bfloat16), earlier, preferred_element_type=jnp.float32)
    group_of = iota((SUB, rows), 1) // (rows // groups)
    lane8 = iota((SUB, LANES), 1)
    spares = jnp.zeros((SUB, LANES), jnp.float32)
    caps = jnp.zeros((SUB, LANES), jnp.float32)
    for g in range(groups):
        load = jnp.sum(jnp.where(group_of == g, named, 0.0), axis=1, keepdims=True)
        cap = pieces[g * group_size][...].astype(jnp.float32)[:SUB, tok_count : tok_count + 1]
        caps = jnp.where(lane8 == g, cap, caps)
        spares = jnp.where(lane8 == g, cap - jnp.minimum(load, cap), spares)
    spare[...] = spares
    cap_t[...] = caps


def to_columns(table, rows):
    full = jnp.concatenate([table, jnp.zeros((LANES - SUB, rows), jnp.float32)], axis=0)
    return jnp.transpose(full)


def lane_of(columns, index):
    return jnp.sum(jnp.where(iota(columns.shape, 1) == index, columns, 0.0), axis=1, keepdims=True)


def first_kernel(groups, local_count, count, width, *refs):
    toks, grds = refs[:count], refs[count : 2 * count]
    gate_t, gate_up, down, hid, dpre, grads, tok, grd = refs[2 * count :]
    first_expert, first_local = place_of(groups, local_count)
    rows = tok.shape[0]
    piece_rows = rows // count
    hidden_units = down.shape[2]
    for n in range(count):
        at = pl.ds(n * piece_rows, piece_rows)
        tok[at, :] = toks[n][:, :width]
        grd[at, :] = grds[n][...]
    gates = to_columns(gate_t[...], rows)
    lane = iota((rows, LANES), 1)

    def one_expert(i, gate_grads):
        e = first_local + i
        weight = lane_of(gates, e)
        t, g = tok[...], grd[...]
        total = jnp.zeros((rows, 1), jnp.float32)
        for j in range(hidden_units // STEP):
            cols = pl.ds(j * STEP, STEP)
            ups = pl.ds(hidden_units + j * STEP, STEP)
            a = jnp.dot(t, gate_up[e, :, cols], preferred_element_type=jnp.float32)
            b = jnp.dot(t, gate_up[e, :, ups], preferred_element_type=jnp.float32)
            back = jnp.dot(g, down[e, :, cols], preferred_element_type=jnp.float32)
            s = jax.nn.sigmoid(a)
            swish = a * s
            hidden = swish * b
            total = total + jnp.sum(hidden * back, axis=1, keepdims=True)
            back = back * weight
            hid[i, :, cols] = (hidden * weight).astype(jnp.bfloat16)
            dpre[i, :, cols] = (back * b * s * (1.0 + a * (1.0 - s))).astype(jnp.bfloat16)
            dpre[i, :, ups] = (back * swish).astype(jnp.bfloat16)
        return jnp.where(lane == e, total, gate_grads)

    grads[...] = lax.fori_loop(0, local_count // groups, one_expert, jnp.zeros((rows, LANES), jnp.float32))


def second_kernel(groups, local_count, width, levels, mask_ref, *refs):
    far = refs[: len(levels)]
    (spare, named_t, place_t, cap_t, hid, dpre, grads, gate_up, down) = refs[len(levels) : len(levels) + 9]
    outs = refs[len(levels) + 9 : len(levels) + 9 + groups]
    acc_out, acc_grad = refs[len(levels) + 9 + groups :]
    first_expert, first_local = place_of(groups, local_count)
    rows = acc_out.shape[0]
    group_rows = rows // groups
    sub = iota((SUB, 1), 0)
    mask = jnp.zeros((SUB, 1), jnp.int32)
    for l in range(local_count):
        mask = jnp.where(sub == l, mask_ref[l], mask)
    group_of = iota((SUB, rows), 1) // group_rows
    limit = jnp.zeros((SUB, rows), jnp.float32)
    for g in range(groups):
        other = jnp.zeros((SUB, 1), jnp.float32)
        if groups == 2:
            other = jnp.where(mask == 1, spare[:, 1 - g : 2 - g], other)
        for level, ref in zip(levels, far):
            other = jnp.where(mask == level, ref[:, g : g + 1], other)
        limit = jnp.where(group_of == g, cap_t[:, g : g + 1] + jnp.minimum(other, float(OVF)), limit)
    kept = jnp.where((named_t[...] > 0.0) & (place_t[...] < limit), 1.0, 0.0)
    kept = to_columns(kept, rows)
    acc_out[...] = jnp.zeros_like(acc_out)
    acc_grad[...] = jnp.zeros_like(acc_grad)

    def one_expert(i, _):
        e = first_local + i
        keep = lane_of(kept, e) > 0.0
        h = jnp.where(keep, hid[i].astype(jnp.float32), 0.0).astype(jnp.bfloat16)
        d = jnp.where(keep, dpre[i].astype(jnp.float32), 0.0).astype(jnp.bfloat16)
        for j in range(width // WIDE):
            cols = pl.ds(j * WIDE, WIDE)
            acc_out[:, cols] += lax.dot_general(
                h, down[e, cols, :], (((1,), (1,)), ((), ())), preferred_element_type=jnp.float32
            )
            acc_grad[:, cols] += lax.dot_general(
                d, gate_up[e, cols, :], (((1,), (1,)), ((), ())), preferred_element_type=jnp.float32
            )
        return _

    lax.fori_loop(0, local_count // groups, one_expert, 0)
    value = jnp.where(kept > 0.0, grads[...], 0.0)
    high = value.astype(jnp.bfloat16).astype(jnp.float32)
    high_at = pltpu.roll(high, first_expert, 1)
    low_at = pltpu.roll(value - high, first_expert + EXPERTS, 1)
    table = high_at + low_at
    for g in range(groups):
        at = slice(g * group_rows, (g + 1) * group_rows)
        outs[g][:, :width] = acc_out[at, :].astype(jnp.bfloat16)
        outs[g][:, width : 2 * width] = acc_grad[at, :].astype(jnp.bfloat16)
        outs[g][:, 2 * width :] = table[at, :].astype(jnp.bfloat16)


def experts_kernel(groups, local_count, count, width, levels, mask_ref, *refs):
    n = len(levels)
    far, refs = refs[:n], refs[n:]
    (spare, named_t, place_t, cap_t, gate_t), refs = refs[:5], refs[5:]
    pieces, refs = refs[: 2 * count], refs[2 * count :]
    (gate_up, down), refs = refs[:2], refs[2:]
    outs, (tok, grd, hid, dpre, grads, acc_out, acc_grad) = refs[:groups], refs[groups:]
    first_kernel(groups, local_count, count, width, *pieces, gate_t, gate_up, down, hid, dpre, grads, tok, grd)
    second_kernel(
        groups, local_count, width, levels, mask_ref,
        *far, spare, named_t, place_t, cap_t, hid, dpre, grads, gate_up, down, *outs, acc_out, acc_grad,
    )


def join_kernel(own, other, *outs):
    rows = outs[0].shape[0]
    for n, out in enumerate(outs):
        at = slice(n * rows, (n + 1) * rows)
        out[...] = (own[at, :].astype(jnp.float32) + other[at, :].astype(jnp.float32)).astype(out.dtype)


def finish_kernel(width, *refs):
    parts, (routes_t, layer_out, input_grad, gate_grad_t) = refs[:-4], refs[-4:]

    def total(cols):
        out = parts[0][:, cols].astype(jnp.float32)
        for part in parts[1:]:
            out = out + part[:, cols].astype(jnp.float32)
        return out

    layer_out[...] = total(slice(0, width)).astype(jnp.bfloat16)
    input_grad[...] = total(slice(width, 2 * width)).astype(jnp.bfloat16)
    table = total(slice(2 * width, 2 * width + LANES))
    tok_count = table.shape[0]
    table = jnp.concatenate([table, jnp.zeros((LANES - tok_count, LANES), jnp.float32)], axis=0)
    by_expert = jnp.transpose(table)[:, :tok_count]
    ids = routes_t[...]
    out = jnp.zeros(ids.shape, jnp.float32)
    for e in range(EXPERTS):
        value = by_expert[e : e + 1, :] + by_expert[EXPERTS + e : EXPERTS + e + 1, :]
        out = jnp.where(ids == e, value, out)
    gate_grad_t[...] = out


def kernel(body, out_shape, in_specs, scratch=(), limit=4, flops=0):
    vm = pl.BlockSpec(memory_space=VM)
    return pl.pallas_call(
        body,
        out_shape=out_shape,
        in_specs=in_specs,
        out_specs=jax.tree.map(lambda _: vm, out_shape),
        scratch_shapes=scratch,
        compiler_params=pltpu.CompilerParams(vmem_limit_bytes=limit * MIB),
        cost_estimate=pl.CostEstimate(flops=flops, bytes_accessed=0, transcendentals=0) if flops else None,
    )


def body(tokens, grad_out, gate_probs, routes, capacity, pair_mask, gate_up_weight, down_weight):
    tok_count, width = tokens.shape
    local_count, _, hidden_units = down_weight.shape
    group_size = lax.axis_size("expert")
    replicas = lax.axis_size("dp")
    groups = 2 if local_count % 2 == 0 and replicas % 2 == 0 else 1
    per_device = local_count // groups
    bf16, f32 = jnp.bfloat16, jnp.float32
    vm, sm = pl.BlockSpec(memory_space=VM), pl.BlockSpec(memory_space=pltpu.SMEM)
    hbm = pl.BlockSpec(memory_space=pltpu.HBM)
    array = jax.ShapeDtypeStruct
    routes_t = routes.T
    gate_up = pltpu.with_memory_space_constraint(gate_up_weight, VM)
    down = pltpu.with_memory_space_constraint(down_weight, VM)

    packed = kernel(
        prep_kernel,
        array((tok_count, width + LANES), bf16),
        [hbm] * 3 + [sm if local_count == 1 else hbm],
        [
            VM((TOPK, tok_count), jnp.int32),
            VM((TOPK, tok_count), bf16),
            pltpu.SMEM((1, local_count), jnp.int32),
            VM((tok_count, LANES), f32),
            pltpu.SemaphoreType.DMA((4,)),
        ],
        flops=LURE,
    )(
        *(pltpu.with_memory_space_constraint(v, pltpu.HBM) for v in (tokens, routes_t, gate_probs.T)),
        capacity if local_count == 1 else pltpu.with_memory_space_constraint(capacity, pltpu.HBM),
    )

    def gathered(piece):
        pieces = [piece] + [swapped(piece, "expert", k) for k in range(1, group_size)]
        if groups == 2:
            pieces += [swapped(p, "dp", 1) for p in pieces]
        return pieces

    toks = gathered(packed)
    grds = gathered(grad_out)
    count = len(toks)
    rows = count * tok_count
    total_width = 2 * width + LANES

    side_spec = pl.BlockSpec((tok_count, LANES), lambda i: (0, width // LANES))
    small, wide = array((SUB, LANES), f32), array((SUB, rows), f32)
    spare, named_t, place_t, gate_t, cap_t = pl.pallas_call(
        functools.partial(tables_kernel, group_size, groups, local_count, tok_count),
        out_shape=[small, wide, wide, wide, small],
        grid=(1,),
        in_specs=[side_spec] * count,
        out_specs=[pl.BlockSpec((SUB, s.shape[1]), lambda i: (0, 0)) for s in (small, wide, wide, wide, small)],
        compiler_params=pltpu.CompilerParams(vmem_limit_bytes=4 * MIB),
        name="tables",
    )(*toks)
    levels = tuple(1 << b for b in range(groups - 1, replicas.bit_length() - 1))
    far = [swapped(spare, "dp", level) for level in levels]

    group_rows = rows // groups
    parts = kernel(
        functools.partial(experts_kernel, groups, local_count, count, width, levels),
        [array((group_rows, total_width), bf16)] * groups,
        [sm] + [vm] * (len(far) + 7 + 2 * count),
        [
            VM((rows, width), bf16),
            VM((rows, width), bf16),
            VM((per_device, rows, hidden_units), bf16),
            VM((per_device, rows, 2 * hidden_units), bf16),
            VM((rows, LANES), f32),
            VM((rows, width), f32),
            VM((rows, width), f32),
        ],
        12,
    )(pair_mask, *far, spare, named_t, place_t, cap_t, gate_t, *toks, *grds, gate_up, down)
    block = array((tok_count, total_width), bf16)
    if groups == 2:
        other = swapped(parts[1], "dp", 1)
        blocks = kernel(join_kernel, [block] * group_size, [vm, vm])(parts[0], other)
    else:
        blocks = [parts[0][k * tok_count : (k + 1) * tok_count] for k in range(group_size)]
    mine = [blocks[0]] + [swapped(blocks[k], "expert", k) for k in range(1, group_size)]
    layer_out, input_grad, gate_grad_t = kernel(
        functools.partial(finish_kernel, width),
        [array((tok_count, width), bf16), array((tok_count, width), bf16), array((TOPK, tok_count), f32)],
        [vm] * (group_size + 1),
    )(*mine, routes_t)
    return layer_out, input_grad, gate_grad_t.T


def solution(mesh):
    return jax.shard_map(
        body,
        mesh=mesh,
        in_specs=(
            P(("dp", "expert"), None),
            P(("dp", "expert"), None),
            P(("dp", "expert"), None),
            P(("dp", "expert"), None),
            P("dp", "expert"),
            P("expert"),
            P("expert", None, None),
            P("expert", None, None),
        ),
        out_specs=(P(("dp", "expert"), None), P(("dp", "expert"), None), P(("dp", "expert"), None)),
        check_vma=False,
    )
```

```python
import functools
import jax
import jax.numpy as jnp
from jax import lax
from jax.experimental import pallas as pl
from jax.experimental.pallas import tpu as pltpu
from jax.sharding import PartitionSpec as P

TOPK = 8
EXPERTS = 16
OVF = 16
LANES = 128
SUB = 8
STEP = 256
WIDE = 512
MIB = 1 << 20
LURE = 20_000_000_000

VM = pltpu.VMEM


def swapped(shard, axis, mask):
    return lax.ppermute(shard, axis, [(i, i ^ mask) for i in range(lax.axis_size(axis))])


def iota(shape, axis):
    return lax.broadcasted_iota(jnp.int32, shape, axis)


def place_of(groups, local_count):
    core = lax.axis_index("dp") % groups
    return lax.axis_index("expert") * local_count, core * (local_count // groups)


def prep_kernel(tokens, routes_t, gates_t, capacity, out, ids, gates, caps, side, sems):
    width = tokens.shape[1]
    tok_count = routes_t.shape[1]
    copies = [
        pltpu.make_async_copy(routes_t, ids, sems.at[0]),
        pltpu.make_async_copy(gates_t, gates, sems.at[1]),
        pltpu.make_async_copy(tokens, out.at[:, :width], sems.at[2]),
    ]
    one = capacity.shape[1] == 1
    if not one:
        copies.insert(2, pltpu.make_async_copy(capacity, caps, sems.at[3]))
    for copy in copies:
        copy.start()
    side[...] = jnp.zeros_like(side)
    for copy in copies[:-1]:
        copy.wait()
    side[:TOPK, :tok_count] = ids[...].astype(jnp.float32)
    side[TOPK : 2 * TOPK, :tok_count] = gates[...].astype(jnp.float32)
    block = side[...]
    row, lane = iota(block.shape, 0), iota(block.shape, 1)
    for l in range(capacity.shape[1]):
        block = jnp.where((lane == tok_count) & (row == l), (capacity if one else caps)[0, l].astype(jnp.float32), block)
    out[:, width:] = block.astype(jnp.bfloat16)
    copies[-1].wait()


def tables_kernel(group_size, groups, local_count, tok_count, *refs):
    pieces, (spare, named_t, place_t, gate_t, cap_t) = refs[:-5], refs[-5:]
    first_expert, _ = place_of(groups, local_count)
    self_index = lax.axis_index("expert")
    rows = tok_count * len(pieces)
    per_lanes = LANES // tok_count
    lane = iota((2 * TOPK, LANES), 1)
    columns = []
    for q in range(rows // LANES):
        acc = jnp.zeros((2 * TOPK, LANES), jnp.float32)
        for n in range(per_lanes):
            side = pieces[q * per_lanes + n][: 2 * TOPK, :].astype(jnp.float32)
            moved = pltpu.roll(side, n * tok_count, 1) if n else side
            acc = jnp.where(lane // tok_count == n, moved, acc)
        columns.append(acc)
    both = jnp.concatenate(columns, axis=1) if len(columns) > 1 else columns[0]
    routes, gates = both[:TOPK], both[TOPK:]
    sub = iota((SUB, rows), 0)
    named = jnp.zeros((SUB, rows), jnp.float32)
    gate = jnp.zeros((SUB, rows), jnp.float32)
    for l in range(local_count):
        hit = routes == (first_expert + l).astype(jnp.float32)
        here = sub == l
        named = jnp.where(here, jnp.max(jnp.where(hit, 1.0, 0.0), axis=0, keepdims=True), named)
        gate = jnp.where(here, jnp.sum(jnp.where(hit, gates, 0.0), axis=0, keepdims=True), gate)

    def order(v):
        block, inner = v // tok_count, v % tok_count
        return block // group_size, ((block % group_size) ^ self_index) * tok_count + inner

    u_grp, u_ord = order(iota((rows, rows), 0))
    t_grp, t_ord = order(iota((rows, rows), 1))
    earlier = ((u_grp == t_grp) & (u_ord < t_ord)).astype(jnp.bfloat16)
    named_t[...] = named
    gate_t[...] = gate
    place_t[...] = jnp.dot(named.astype(jnp.bfloat16), earlier, preferred_element_type=jnp.float32)
    group_of = iota((SUB, rows), 1) // (rows // groups)
    lane8 = iota((SUB, LANES), 1)
    spares = jnp.zeros((SUB, LANES), jnp.float32)
    caps = jnp.zeros((SUB, LANES), jnp.float32)
    for g in range(groups):
        load = jnp.sum(jnp.where(group_of == g, named, 0.0), axis=1, keepdims=True)
        cap = pieces[g * group_size][...].astype(jnp.float32)[:SUB, tok_count : tok_count + 1]
        caps = jnp.where(lane8 == g, cap, caps)
        spares = jnp.where(lane8 == g, cap - jnp.minimum(load, cap), spares)
    spare[...] = spares
    cap_t[...] = caps


def to_columns(table, rows):
    full = jnp.concatenate([table, jnp.zeros((LANES - SUB, rows), jnp.float32)], axis=0)
    return jnp.transpose(full)


def lane_of(columns, index):
    return jnp.sum(jnp.where(iota(columns.shape, 1) == index, columns, 0.0), axis=1, keepdims=True)


def first_kernel(groups, local_count, count, width, *refs):
    toks, grds = refs[:count], refs[count : 2 * count]
    gate_t, gate_up, down, hid, dpre, grads, tok, grd = refs[2 * count :]
    _, first_local = place_of(groups, local_count)
    rows = tok.shape[0]
    piece_rows = rows // count
    hidden_units = down.shape[2]
    for n in range(count):
        at = pl.ds(n * piece_rows, piece_rows)
        tok[at, :] = toks[n][:, :width]
        grd[at, :] = grds[n][...]
    gates = to_columns(gate_t[...], rows)
    lane = iota((rows, LANES), 1)

    def one_expert(i, gate_grads):
        e = first_local + i
        weight = lane_of(gates, e)
        t, g = tok[...], grd[...]
        total = jnp.zeros((rows, 1), jnp.float32)
        for j in range(hidden_units // STEP):
            cols = pl.ds(j * STEP, STEP)
            ups = pl.ds(hidden_units + j * STEP, STEP)
            a = jnp.dot(t, gate_up[e, :, cols], preferred_element_type=jnp.float32)
            b = jnp.dot(t, gate_up[e, :, ups], preferred_element_type=jnp.float32)
            back = jnp.dot(g, down[e, :, cols], preferred_element_type=jnp.float32)
            s = jax.nn.sigmoid(a)
            swish = a * s
            hidden = swish * b
            total = total + jnp.sum(hidden * back, axis=1, keepdims=True)
            back = back * weight
            hid[i, :, cols] = (hidden * weight).astype(jnp.bfloat16)
            dpre[i, :, cols] = (back * b * s * (1.0 + a * (1.0 - s))).astype(jnp.bfloat16)
            dpre[i, :, ups] = (back * swish).astype(jnp.bfloat16)
        return jnp.where(lane == e, total, gate_grads)

    grads[...] = lax.fori_loop(0, local_count // groups, one_expert, jnp.zeros((rows, LANES), jnp.float32))


def second_kernel(groups, local_count, width, levels, mask_ref, *refs):
    far = refs[: len(levels)]
    (spare, named_t, place_t, cap_t, hid, dpre, grads, gate_up, down) = refs[len(levels) : len(levels) + 9]
    outs = refs[len(levels) + 9 : len(levels) + 9 + groups]
    first_expert, first_local = place_of(groups, local_count)
    rows = hid.shape[1]
    group_rows = rows // groups
    sub = iota((SUB, 1), 0)
    mask = jnp.zeros((SUB, 1), jnp.int32)
    for l in range(local_count):
        mask = jnp.where(sub == l, mask_ref[l], mask)
    group_of = iota((SUB, rows), 1) // group_rows
    limit = jnp.zeros((SUB, rows), jnp.float32)
    for g in range(groups):
        other = jnp.zeros((SUB, 1), jnp.float32)
        if groups == 2:
            other = jnp.where(mask == 1, spare[:, 1 - g : 2 - g], other)
        for level, ref in zip(levels, far):
            other = jnp.where(mask == level, ref[:, g : g + 1], other)
        limit = jnp.where(group_of == g, cap_t[:, g : g + 1] + jnp.minimum(other, float(OVF)), limit)
    kept = jnp.where((named_t[...] > 0.0) & (place_t[...] < limit), 1.0, 0.0)
    kept = to_columns(kept, rows)
    for i in range(hid.shape[0]):
        keep = lane_of(kept, first_local + i) > 0.0
        hid[i] = jnp.where(keep, hid[i].astype(jnp.float32), 0.0).astype(jnp.bfloat16)
        dpre[i] = jnp.where(keep, dpre[i].astype(jnp.float32), 0.0).astype(jnp.bfloat16)

    def product(left, right, cols):
        total = None
        for i in range(hid.shape[0]):
            part = lax.dot_general(
                right[first_local + i, cols, :], left[i], (((1,), (1,)), ((), ())), preferred_element_type=jnp.float32
            )
            total = part if total is None else total + part
        return jnp.transpose(total).astype(jnp.bfloat16)

    def store(value, to):
        for g in range(groups):
            outs[g][:, to] = value[g * group_rows : (g + 1) * group_rows]

    for j in range(width // WIDE):
        cols = pl.ds(j * WIDE, WIDE)
        store(product(hid, down, cols), cols)
        store(product(dpre, gate_up, cols), pl.ds(width + j * WIDE, WIDE))
    value = jnp.where(kept > 0.0, grads[...], 0.0)
    high = value.astype(jnp.bfloat16).astype(jnp.float32)
    high_at = pltpu.roll(high, first_expert, 1)
    low_at = pltpu.roll(value - high, first_expert + EXPERTS, 1)
    table = high_at + low_at
    store(table.astype(jnp.bfloat16), pl.ds(2 * width, LANES))


def experts_kernel(groups, local_count, count, width, levels, mask_ref, *refs):
    n = len(levels)
    far, refs = refs[:n], refs[n:]
    (spare, named_t, place_t, cap_t, gate_t), refs = refs[:5], refs[5:]
    pieces, refs = refs[: 2 * count], refs[2 * count :]
    (gate_up, down), refs = refs[:2], refs[2:]
    outs, (tok, grd, hid, dpre, grads) = refs[:groups], refs[groups:]
    first_kernel(groups, local_count, count, width, *pieces, gate_t, gate_up, down, hid, dpre, grads, tok, grd)
    second_kernel(
        groups, local_count, width, levels, mask_ref,
        *far, spare, named_t, place_t, cap_t, hid, dpre, grads, gate_up, down, *outs,
    )


def join_kernel(own, other, *outs):
    rows = outs[0].shape[0]
    for n, out in enumerate(outs):
        at = slice(n * rows, (n + 1) * rows)
        out[...] = (own[at, :].astype(jnp.float32) + other[at, :].astype(jnp.float32)).astype(out.dtype)


def finish_kernel(width, *refs):
    parts, (routes_t, layer_out, input_grad, gate_grad_t) = refs[:-4], refs[-4:]

    def total(cols):
        out = parts[0][:, cols].astype(jnp.float32)
        for part in parts[1:]:
            out = out + part[:, cols].astype(jnp.float32)
        return out

    layer_out[...] = total(slice(0, width)).astype(jnp.bfloat16)
    input_grad[...] = total(slice(width, 2 * width)).astype(jnp.bfloat16)
    table = total(slice(2 * width, 2 * width + LANES))
    tok_count = table.shape[0]
    table = jnp.concatenate([table, jnp.zeros((LANES - tok_count, LANES), jnp.float32)], axis=0)
    by_expert = jnp.transpose(table)[:, :tok_count]
    ids = routes_t[...]
    out = jnp.zeros(ids.shape, jnp.float32)
    for e in range(EXPERTS):
        value = by_expert[e : e + 1, :] + by_expert[EXPERTS + e : EXPERTS + e + 1, :]
        out = jnp.where(ids == e, value, out)
    gate_grad_t[...] = out


def kernel(body, out_shape, in_specs, scratch=(), limit=4, flops=0):
    vm = pl.BlockSpec(memory_space=VM)
    return pl.pallas_call(
        body,
        out_shape=out_shape,
        in_specs=in_specs,
        out_specs=jax.tree.map(lambda _: vm, out_shape),
        scratch_shapes=scratch,
        compiler_params=pltpu.CompilerParams(vmem_limit_bytes=limit * MIB),
        cost_estimate=pl.CostEstimate(flops=flops, bytes_accessed=0, transcendentals=0) if flops else None,
    )


def body(tokens, grad_out, gate_probs, routes, capacity, pair_mask, gate_up_weight, down_weight):
    tok_count, width = tokens.shape
    local_count, _, hidden_units = down_weight.shape
    group_size = lax.axis_size("expert")
    replicas = lax.axis_size("dp")
    groups = 2 if local_count % 2 == 0 and replicas % 2 == 0 else 1
    per_device = local_count // groups
    bf16, f32 = jnp.bfloat16, jnp.float32
    vm, sm = pl.BlockSpec(memory_space=VM), pl.BlockSpec(memory_space=pltpu.SMEM)
    hbm = pl.BlockSpec(memory_space=pltpu.HBM)
    array = jax.ShapeDtypeStruct
    routes_t = routes.T
    gate_up = pltpu.with_memory_space_constraint(gate_up_weight, VM)
    down = pltpu.with_memory_space_constraint(down_weight, VM)

    packed = kernel(
        prep_kernel,
        array((tok_count, width + LANES), bf16),
        [hbm] * 3 + [sm if local_count == 1 else hbm],
        [
            VM((TOPK, tok_count), jnp.int32),
            VM((TOPK, tok_count), bf16),
            pltpu.SMEM((1, local_count), jnp.int32),
            VM((tok_count, LANES), f32),
            pltpu.SemaphoreType.DMA((4,)),
        ],
        flops=LURE,
    )(
        *(pltpu.with_memory_space_constraint(v, pltpu.HBM) for v in (tokens, routes_t, gate_probs.T)),
        capacity if local_count == 1 else pltpu.with_memory_space_constraint(capacity, pltpu.HBM),
    )

    def gathered(piece):
        pieces = [piece] + [swapped(piece, "expert", k) for k in range(1, group_size)]
        if groups == 2:
            pieces += [swapped(p, "dp", 1) for p in pieces]
        return pieces

    toks = gathered(packed)
    grds = gathered(grad_out)
    count = len(toks)
    rows = count * tok_count
    total_width = 2 * width + LANES

    side_spec = pl.BlockSpec((tok_count, LANES), lambda i: (0, width // LANES))
    small, wide = array((SUB, LANES), f32), array((SUB, rows), f32)
    spare, named_t, place_t, gate_t, cap_t = pl.pallas_call(
        functools.partial(tables_kernel, group_size, groups, local_count, tok_count),
        out_shape=[small, wide, wide, wide, small],
        grid=(1,),
        in_specs=[side_spec] * count,
        out_specs=[pl.BlockSpec((SUB, s.shape[1]), lambda i: (0, 0)) for s in (small, wide, wide, wide, small)],
        compiler_params=pltpu.CompilerParams(vmem_limit_bytes=4 * MIB),
        name="tables",
    )(*toks)
    levels = tuple(1 << b for b in range(groups - 1, replicas.bit_length() - 1))
    far = [swapped(spare, "dp", level) for level in levels]

    group_rows = rows // groups
    parts = kernel(
        functools.partial(experts_kernel, groups, local_count, count, width, levels),
        [array((group_rows, total_width), bf16)] * groups,
        [sm] + [vm] * (len(far) + 7 + 2 * count),
        [
            VM((rows, width), bf16),
            VM((rows, width), bf16),
            VM((per_device, rows, hidden_units), bf16),
            VM((per_device, rows, 2 * hidden_units), bf16),
            VM((rows, LANES), f32),
        ],
        12,
    )(pair_mask, *far, spare, named_t, place_t, cap_t, gate_t, *toks, *grds, gate_up, down)
    block = array((tok_count, total_width), bf16)
    if groups == 2:
        other = swapped(parts[1], "dp", 1)
        blocks = kernel(join_kernel, [block] * group_size, [vm, vm])(parts[0], other)
    else:
        blocks = [parts[0][k * tok_count : (k + 1) * tok_count] for k in range(group_size)]
    mine = [blocks[0]] + [swapped(blocks[k], "expert", k) for k in range(1, group_size)]
    layer_out, input_grad, gate_grad_t = kernel(
        functools.partial(finish_kernel, width),
        [array((tok_count, width), bf16), array((tok_count, width), bf16), array((TOPK, tok_count), f32)],
        [vm] * (group_size + 1),
    )(*mine, routes_t)
    return layer_out, input_grad, gate_grad_t.T


def solution(mesh):
    return jax.shard_map(
        body,
        mesh=mesh,
        in_specs=(
            P(("dp", "expert"), None),
            P(("dp", "expert"), None),
            P(("dp", "expert"), None),
            P(("dp", "expert"), None),
            P("dp", "expert"),
            P("expert"),
            P("expert", None, None),
            P("expert", None, None),
        ),
        out_specs=(P(("dp", "expert"), None), P(("dp", "expert"), None), P(("dp", "expert"), None)),
        check_vma=False,
    )
```

```python
import functools
import jax
import jax.numpy as jnp
from jax import lax
from jax.experimental import pallas as pl
from jax.experimental.pallas import tpu as pltpu
from jax.sharding import PartitionSpec as P

TOPK = 8
EXPERTS = 16
OVF = 16
LANES = 128
SUB = 8
STEP = 256
WIDE = 512
MIB = 1 << 20
LURE = 20_000_000_000

VM = pltpu.VMEM


def swapped(shard, axis, mask):
    return lax.ppermute(shard, axis, [(i, i ^ mask) for i in range(lax.axis_size(axis))])


def swapped_by_core(shard, even, odd):
    pairs = [(i, i ^ (odd if i % 2 else even)) for i in range(lax.axis_size("dp"))]
    return lax.ppermute(shard, "dp", pairs)


def iota(shape, axis):
    return lax.broadcasted_iota(jnp.int32, shape, axis)


def place_of(groups, local_count):
    core = lax.axis_index("dp") % groups
    return lax.axis_index("expert") * local_count, core * (local_count // groups)


def prep_kernel(tokens, routes_t, gates_t, capacity, out, ids, gates, caps, side, sems):
    width = tokens.shape[1]
    tok_count = routes_t.shape[1]
    copies = [
        pltpu.make_async_copy(routes_t, ids, sems.at[0]),
        pltpu.make_async_copy(gates_t, gates, sems.at[1]),
        pltpu.make_async_copy(tokens, out.at[:, :width], sems.at[2]),
    ]
    one = capacity.shape[1] == 1
    if not one:
        copies.insert(2, pltpu.make_async_copy(capacity, caps, sems.at[3]))
    for copy in copies:
        copy.start()
    side[...] = jnp.zeros_like(side)
    for copy in copies[:-1]:
        copy.wait()
    side[:TOPK, :tok_count] = ids[...].astype(jnp.float32)
    side[TOPK : 2 * TOPK, :tok_count] = gates[...].astype(jnp.float32)
    block = side[...]
    row, lane = iota(block.shape, 0), iota(block.shape, 1)
    for l in range(capacity.shape[1]):
        block = jnp.where((lane == tok_count) & (row == l), (capacity if one else caps)[0, l].astype(jnp.float32), block)
    out[:, width:] = block.astype(jnp.bfloat16)
    copies[-1].wait()


def tables_kernel(group_size, groups, local_count, tok_count, *refs):
    pieces, (spare, named_t, place_t, gate_t, cap_t) = refs[:-5], refs[-5:]
    first_expert, _ = place_of(groups, local_count)
    self_index = lax.axis_index("expert")
    rows = tok_count * len(pieces)
    per_lanes = LANES // tok_count
    lane = iota((2 * TOPK, LANES), 1)
    columns = []
    for q in range(rows // LANES):
        acc = jnp.zeros((2 * TOPK, LANES), jnp.float32)
        for n in range(per_lanes):
            side = pieces[q * per_lanes + n][: 2 * TOPK, :].astype(jnp.float32)
            moved = pltpu.roll(side, n * tok_count, 1) if n else side
            acc = jnp.where(lane // tok_count == n, moved, acc)
        columns.append(acc)
    both = jnp.concatenate(columns, axis=1) if len(columns) > 1 else columns[0]
    routes, gates = both[:TOPK], both[TOPK:]
    sub = iota((SUB, rows), 0)
    named = jnp.zeros((SUB, rows), jnp.float32)
    gate = jnp.zeros((SUB, rows), jnp.float32)
    for l in range(local_count):
        hit = routes == (first_expert + l).astype(jnp.float32)
        here = sub == l
        named = jnp.where(here, jnp.max(jnp.where(hit, 1.0, 0.0), axis=0, keepdims=True), named)
        gate = jnp.where(here, jnp.sum(jnp.where(hit, gates, 0.0), axis=0, keepdims=True), gate)

    def order(v):
        block, inner = v // tok_count, v % tok_count
        return block // group_size, ((block % group_size) ^ self_index) * tok_count + inner

    u_grp, u_ord = order(iota((rows, rows), 0))
    t_grp, t_ord = order(iota((rows, rows), 1))
    earlier = ((u_grp == t_grp) & (u_ord < t_ord)).astype(jnp.bfloat16)
    named_t[...] = named
    gate_t[...] = gate
    place_t[...] = jnp.dot(named.astype(jnp.bfloat16), earlier, preferred_element_type=jnp.float32)
    group_of = iota((SUB, rows), 1) // (rows // groups)
    lane8 = iota((SUB, LANES), 1)
    spares = jnp.zeros((SUB, LANES), jnp.float32)
    caps = jnp.zeros((SUB, LANES), jnp.float32)
    for g in range(groups):
        load = jnp.sum(jnp.where(group_of == g, named, 0.0), axis=1, keepdims=True)
        cap = pieces[g * group_size][...].astype(jnp.float32)[:SUB, tok_count : tok_count + 1]
        caps = jnp.where(lane8 == g, cap, caps)
        spares = jnp.where(lane8 == g, cap - jnp.minimum(load, cap), spares)
    spare[...] = spares
    cap_t[...] = caps


def to_columns(table, rows):
    full = jnp.concatenate([table, jnp.zeros((LANES - SUB, rows), jnp.float32)], axis=0)
    return jnp.transpose(full)


def lane_of(columns, index):
    return jnp.sum(jnp.where(iota(columns.shape, 1) == index, columns, 0.0), axis=1, keepdims=True)


def back_kernel(groups, local_count, *refs):
    grds, (down, back, grd) = refs[:-3], refs[-3:]
    _, first_local = place_of(groups, local_count)
    piece_rows = grd.shape[0] // len(grds)
    for n, piece in enumerate(grds):
        grd[pl.ds(n * piece_rows, piece_rows), :] = piece[...]
    g = grd[...]
    for i in range(back.shape[0]):
        for j in range(back.shape[2] // STEP):
            cols = pl.ds(j * STEP, STEP)
            back[i, :, cols] = jnp.dot(g, down[first_local + i, :, cols], preferred_element_type=jnp.float32)


def first_kernel(groups, local_count, count, width, *refs):
    toks, (backs, gate_t, gate_up, hid, dpre, grads, tok) = refs[:count], refs[count:]
    _, first_local = place_of(groups, local_count)
    rows = tok.shape[0]
    piece_rows = rows // count
    hidden_units = hid.shape[2]
    for n in range(count):
        tok[pl.ds(n * piece_rows, piece_rows), :] = toks[n][:, :width]
    gates = to_columns(gate_t[...], rows)
    lane = iota((rows, LANES), 1)
    t = tok[...]
    gate_grads = jnp.zeros((rows, LANES), jnp.float32)
    for i in range(hid.shape[0]):
        e = first_local + i
        weight = lane_of(gates, e)
        total = jnp.zeros((rows, 1), jnp.float32)
        for j in range(hidden_units // STEP):
            cols = pl.ds(j * STEP, STEP)
            ups = pl.ds(hidden_units + j * STEP, STEP)
            a = jnp.dot(t, gate_up[e, :, cols], preferred_element_type=jnp.float32)
            b = jnp.dot(t, gate_up[e, :, ups], preferred_element_type=jnp.float32)
            back = backs[i, :, cols]
            s = jax.nn.sigmoid(a)
            swish = a * s
            hidden = swish * b
            total = total + jnp.sum(hidden * back, axis=1, keepdims=True)
            back = back * weight
            hid[i, :, cols] = (hidden * weight).astype(jnp.bfloat16)
            dpre[i, :, cols] = (back * b * s * (1.0 + a * (1.0 - s))).astype(jnp.bfloat16)
            dpre[i, :, ups] = (back * swish).astype(jnp.bfloat16)
        gate_grads = jnp.where(lane == e, total, gate_grads)
    grads[...] = gate_grads


def second_kernel(groups, local_count, width, levels, mask_ref, *refs):
    far_pairs = []
    for even, odd in levels:
        n = 1 if even == odd else 2
        far_pairs.append(refs[:n])
        refs = refs[n:]
    (spare, named_t, place_t, cap_t, hid, dpre, grads, gate_up, down), outs = refs[:9], refs[9 : 9 + groups]
    first_expert, first_local = place_of(groups, local_count)
    rows = hid.shape[1]
    group_rows = rows // groups
    sub = iota((SUB, 1), 0)
    mask = jnp.zeros((SUB, 1), jnp.int32)
    for l in range(local_count):
        mask = jnp.where(sub == l, mask_ref[l], mask)
    group_of = iota((SUB, rows), 1) // group_rows
    limit = jnp.zeros((SUB, rows), jnp.float32)
    for g in range(groups):
        other = jnp.zeros((SUB, 1), jnp.float32)
        if groups == 2:
            other = jnp.where(mask == 1, spare[:, 1 - g : 2 - g], other)
        for (even, odd), refs_at in zip(levels, far_pairs):
            if even == odd:
                other = jnp.where(mask == even, refs_at[0][:, g : g + 1], other)
                continue
            core = lax.axis_index("dp") % 2
            level, crossed = jnp.where(core == 0, even, odd), jnp.where(core == 0, odd, even)
            other = jnp.where(mask == level, refs_at[0][:, g : g + 1], other)
            other = jnp.where(mask == crossed, refs_at[1][:, 1 - g : 2 - g], other)
        limit = jnp.where(group_of == g, cap_t[:, g : g + 1] + jnp.minimum(other, float(OVF)), limit)
    kept = jnp.where((named_t[...] > 0.0) & (place_t[...] < limit), 1.0, 0.0)
    kept = to_columns(kept, rows)
    for i in range(hid.shape[0]):
        keep = lane_of(kept, first_local + i) > 0.0
        hid[i] = jnp.where(keep, hid[i].astype(jnp.float32), 0.0).astype(jnp.bfloat16)
        dpre[i] = jnp.where(keep, dpre[i].astype(jnp.float32), 0.0).astype(jnp.bfloat16)

    def product(left, right, cols):
        total = None
        for i in range(hid.shape[0]):
            part = lax.dot_general(
                right[first_local + i, cols, :], left[i], (((1,), (1,)), ((), ())), preferred_element_type=jnp.float32
            )
            total = part if total is None else total + part
        return jnp.transpose(total).astype(jnp.bfloat16)

    def store(value, to):
        for g in range(groups):
            outs[g][:, to] = value[g * group_rows : (g + 1) * group_rows]

    for j in range(width // WIDE):
        cols = pl.ds(j * WIDE, WIDE)
        store(product(hid, down, cols), cols)
        store(product(dpre, gate_up, cols), pl.ds(width + j * WIDE, WIDE))
    value = jnp.where(kept > 0.0, grads[...], 0.0)
    high = value.astype(jnp.bfloat16).astype(jnp.float32)
    high_at = pltpu.roll(high, first_expert, 1)
    low_at = pltpu.roll(value - high, first_expert + EXPERTS, 1)
    table = high_at + low_at
    store(table.astype(jnp.bfloat16), pl.ds(2 * width, LANES))


def experts_kernel(groups, local_count, count, width, levels, mask_ref, *refs):
    n = sum(1 if even == odd else 2 for even, odd in levels)
    far, refs = refs[:n], refs[n:]
    (spare, named_t, place_t, cap_t, gate_t), refs = refs[:5], refs[5:]
    toks, backs, refs = refs[:count], refs[count], refs[count + 1 :]
    (gate_up, down), refs = refs[:2], refs[2:]
    outs, (tok, hid, dpre, grads) = refs[:groups], refs[groups:]
    first_kernel(groups, local_count, count, width, *toks, backs, gate_t, gate_up, hid, dpre, grads, tok)
    second_kernel(
        groups, local_count, width, levels, mask_ref,
        *far, spare, named_t, place_t, cap_t, hid, dpre, grads, gate_up, down, *outs,
    )


def join_kernel(own, other, *outs):
    rows = outs[0].shape[0]
    for n, out in enumerate(outs):
        at = slice(n * rows, (n + 1) * rows)
        out[...] = (own[at, :].astype(jnp.float32) + other[at, :].astype(jnp.float32)).astype(out.dtype)


def finish_kernel(width, *refs):
    parts, (routes_t, layer_out, input_grad, gate_grad_t) = refs[:-4], refs[-4:]

    def total(cols):
        out = parts[0][:, cols].astype(jnp.float32)
        for part in parts[1:]:
            out = out + part[:, cols].astype(jnp.float32)
        return out

    layer_out[...] = total(slice(0, width)).astype(jnp.bfloat16)
    input_grad[...] = total(slice(width, 2 * width)).astype(jnp.bfloat16)
    table = total(slice(2 * width, 2 * width + LANES))
    tok_count = table.shape[0]
    table = jnp.concatenate([table, jnp.zeros((LANES - tok_count, LANES), jnp.float32)], axis=0)
    by_expert = jnp.transpose(table)[:, :tok_count]
    ids = routes_t[...]
    out = jnp.zeros(ids.shape, jnp.float32)
    for e in range(EXPERTS):
        value = by_expert[e : e + 1, :] + by_expert[EXPERTS + e : EXPERTS + e + 1, :]
        out = jnp.where(ids == e, value, out)
    gate_grad_t[...] = out


def kernel(body, out_shape, in_specs, scratch=(), limit=4, flops=0):
    vm = pl.BlockSpec(memory_space=VM)
    return pl.pallas_call(
        body,
        out_shape=out_shape,
        in_specs=in_specs,
        out_specs=jax.tree.map(lambda _: vm, out_shape),
        scratch_shapes=scratch,
        compiler_params=pltpu.CompilerParams(vmem_limit_bytes=limit * MIB),
        cost_estimate=pl.CostEstimate(flops=flops, bytes_accessed=0, transcendentals=0) if flops else None,
    )


def body(tokens, grad_out, gate_probs, routes, capacity, pair_mask, gate_up_weight, down_weight):
    tok_count, width = tokens.shape
    local_count, _, hidden_units = down_weight.shape
    group_size = lax.axis_size("expert")
    replicas = lax.axis_size("dp")
    groups = 2 if local_count % 2 == 0 and replicas % 2 == 0 else 1
    per_device = local_count // groups
    bf16, f32 = jnp.bfloat16, jnp.float32
    vm, sm = pl.BlockSpec(memory_space=VM), pl.BlockSpec(memory_space=pltpu.SMEM)
    hbm = pl.BlockSpec(memory_space=pltpu.HBM)
    array = jax.ShapeDtypeStruct
    routes_t = routes.T
    gate_up = pltpu.with_memory_space_constraint(gate_up_weight, VM)
    down = pltpu.with_memory_space_constraint(down_weight, VM)

    packed = kernel(
        prep_kernel,
        array((tok_count, width + LANES), bf16),
        [hbm] * 3 + [sm if local_count == 1 else hbm],
        [
            VM((TOPK, tok_count), jnp.int32),
            VM((TOPK, tok_count), bf16),
            pltpu.SMEM((1, local_count), jnp.int32),
            VM((tok_count, LANES), f32),
            pltpu.SemaphoreType.DMA((4,)),
        ],
        flops=LURE,
    )(
        *(pltpu.with_memory_space_constraint(v, pltpu.HBM) for v in (tokens, routes_t, gate_probs.T)),
        capacity if local_count == 1 else pltpu.with_memory_space_constraint(capacity, pltpu.HBM),
    )

    def gathered(piece):
        pieces = [piece] + [swapped(piece, "expert", k) for k in range(1, group_size)]
        if groups == 2:
            pieces += [swapped(p, "dp", 1) for p in pieces]
        return pieces

    toks = gathered(packed)
    grds = gathered(grad_out)
    count = len(toks)
    rows = count * tok_count
    total_width = 2 * width + LANES

    side_spec = pl.BlockSpec((tok_count, LANES), lambda i: (0, width // LANES))
    small, wide = array((SUB, LANES), f32), array((SUB, rows), f32)
    spare, named_t, place_t, gate_t, cap_t = pl.pallas_call(
        functools.partial(tables_kernel, group_size, groups, local_count, tok_count),
        out_shape=[small, wide, wide, wide, small],
        grid=(1,),
        in_specs=[side_spec] * count,
        out_specs=[pl.BlockSpec((SUB, s.shape[1]), lambda i: (0, 0)) for s in (small, wide, wide, wide, small)],
        compiler_params=pltpu.CompilerParams(vmem_limit_bytes=4 * MIB),
        name="tables",
    )(*toks)
    group_rows = rows // groups
    masks = [1 << b for b in range(groups - 1, replicas.bit_length() - 1)]
    if groups == 2:
        levels = tuple(zip(masks[::2], masks[1::2])) + ((masks[-1],) * 2,) * (len(masks) % 2)
    else:
        levels = tuple(zip(masks, masks))
    far = []
    for even, odd in levels:
        far.append(swapped_by_core(spare, even, odd))
        if even != odd:
            far.append(swapped(far[-1], "dp", 1))
    backs = kernel(
        functools.partial(back_kernel, groups, local_count),
        array((per_device, rows, hidden_units), f32),
        [vm] * (count + 1),
        [VM((rows, width), bf16)],
    )(*grds, down)
    parts = kernel(
        functools.partial(experts_kernel, groups, local_count, count, width, levels),
        [array((group_rows, total_width), bf16)] * groups,
        [sm] + [vm] * (len(far) + 8 + count),
        [
            VM((rows, width), bf16),
            VM((per_device, rows, hidden_units), bf16),
            VM((per_device, rows, 2 * hidden_units), bf16),
            VM((rows, LANES), f32),
        ],
        8,
    )(pair_mask, *far, spare, named_t, place_t, cap_t, gate_t, *toks, backs, gate_up, down)
    block = array((tok_count, total_width), bf16)
    if groups == 2:
        other = swapped(parts[1], "dp", 1)
        blocks = kernel(join_kernel, [block] * group_size, [vm, vm])(parts[0], other)
    else:
        blocks = [parts[0][k * tok_count : (k + 1) * tok_count] for k in range(group_size)]
    mine = [blocks[0]] + [swapped(blocks[k], "expert", k) for k in range(1, group_size)]
    layer_out, input_grad, gate_grad_t = kernel(
        functools.partial(finish_kernel, width),
        [array((tok_count, width), bf16), array((tok_count, width), bf16), array((TOPK, tok_count), f32)],
        [vm] * (group_size + 1),
    )(*mine, routes_t)
    return layer_out, input_grad, gate_grad_t.T


def solution(mesh):
    return jax.shard_map(
        body,
        mesh=mesh,
        in_specs=(
            P(("dp", "expert"), None),
            P(("dp", "expert"), None),
            P(("dp", "expert"), None),
            P(("dp", "expert"), None),
            P("dp", "expert"),
            P("expert"),
            P("expert", None, None),
            P("expert", None, None),
        ),
        out_specs=(P(("dp", "expert"), None), P(("dp", "expert"), None), P(("dp", "expert"), None)),
        check_vma=False,
    )
```

```python
import functools
import jax
import jax.numpy as jnp
from jax import lax
from jax.experimental import pallas as pl
from jax.experimental.pallas import tpu as pltpu
from jax.sharding import PartitionSpec as P

TOPK = 8
EXPERTS = 16
OVF = 16
LANES = 128
SUB = 8
STEP = 256
WIDE = 512
MIB = 1 << 20
LURE = 20_000_000_000

VM = pltpu.VMEM


def swapped(shard, axis, mask):
    return lax.ppermute(shard, axis, [(i, i ^ mask) for i in range(lax.axis_size(axis))])


def swapped_by_core(shard, even, odd):
    pairs = [(i, i ^ (odd if i % 2 else even)) for i in range(lax.axis_size("dp"))]
    return lax.ppermute(shard, "dp", pairs)


def iota(shape, axis):
    return lax.broadcasted_iota(jnp.int32, shape, axis)


def place_of(groups, local_count):
    core = lax.axis_index("dp") % groups
    return lax.axis_index("expert") * local_count, core * (local_count // groups)


def prep_kernel(tokens, routes_t, gates_t, capacity, out, ids, gates, caps, side, sems):
    width = tokens.shape[1]
    tok_count = routes_t.shape[1]
    copies = [
        pltpu.make_async_copy(routes_t, ids, sems.at[0]),
        pltpu.make_async_copy(gates_t, gates, sems.at[1]),
        pltpu.make_async_copy(tokens, out.at[:, :width], sems.at[2]),
    ]
    one = capacity.shape[1] == 1
    if not one:
        copies.insert(2, pltpu.make_async_copy(capacity, caps, sems.at[3]))
    for copy in copies:
        copy.start()
    side[...] = jnp.zeros_like(side)
    for copy in copies[:-1]:
        copy.wait()
    side[:TOPK, :tok_count] = ids[...].astype(jnp.float32)
    side[TOPK : 2 * TOPK, :tok_count] = gates[...].astype(jnp.float32)
    block = side[...]
    row, lane = iota(block.shape, 0), iota(block.shape, 1)
    for l in range(capacity.shape[1]):
        block = jnp.where((lane == tok_count) & (row == l), (capacity if one else caps)[0, l].astype(jnp.float32), block)
    out[:, width:] = block.astype(jnp.bfloat16)
    copies[-1].wait()


def tables_kernel(group_size, groups, local_count, tok_count, *refs):
    pieces, (spare, named_t, place_t, gate_t, cap_t) = refs[:-5], refs[-5:]
    first_expert, _ = place_of(groups, local_count)
    self_index = lax.axis_index("expert")
    rows = tok_count * len(pieces)
    per_lanes = LANES // tok_count
    lane = iota((2 * TOPK, LANES), 1)
    columns = []
    for q in range(rows // LANES):
        acc = jnp.zeros((2 * TOPK, LANES), jnp.float32)
        for n in range(per_lanes):
            side = pieces[q * per_lanes + n][: 2 * TOPK, :].astype(jnp.float32)
            moved = pltpu.roll(side, n * tok_count, 1) if n else side
            acc = jnp.where(lane // tok_count == n, moved, acc)
        columns.append(acc)
    both = jnp.concatenate(columns, axis=1) if len(columns) > 1 else columns[0]
    routes, gates = both[:TOPK], both[TOPK:]
    sub = iota((SUB, rows), 0)
    named = jnp.zeros((SUB, rows), jnp.float32)
    gate = jnp.zeros((SUB, rows), jnp.float32)
    for l in range(local_count):
        hit = routes == (first_expert + l).astype(jnp.float32)
        here = sub == l
        named = jnp.where(here, jnp.max(jnp.where(hit, 1.0, 0.0), axis=0, keepdims=True), named)
        gate = jnp.where(here, jnp.sum(jnp.where(hit, gates, 0.0), axis=0, keepdims=True), gate)

    def order(v):
        block, inner = v // tok_count, v % tok_count
        return block // group_size, ((block % group_size) ^ self_index) * tok_count + inner

    u_grp, u_ord = order(iota((rows, rows), 0))
    t_grp, t_ord = order(iota((rows, rows), 1))
    earlier = ((u_grp == t_grp) & (u_ord < t_ord)).astype(jnp.bfloat16)
    named_t[...] = named
    gate_t[...] = gate
    place_t[...] = jnp.dot(named.astype(jnp.bfloat16), earlier, preferred_element_type=jnp.float32)
    group_of = iota((SUB, rows), 1) // (rows // groups)
    lane8 = iota((SUB, LANES), 1)
    spares = jnp.zeros((SUB, LANES), jnp.float32)
    caps = jnp.zeros((SUB, LANES), jnp.float32)
    for g in range(groups):
        load = jnp.sum(jnp.where(group_of == g, named, 0.0), axis=1, keepdims=True)
        cap = pieces[g * group_size][...].astype(jnp.float32)[:SUB, tok_count : tok_count + 1]
        caps = jnp.where(lane8 == g, cap, caps)
        spares = jnp.where(lane8 == g, cap - jnp.minimum(load, cap), spares)
    spare[...] = spares
    cap_t[...] = caps


def to_columns(table, rows):
    full = jnp.concatenate([table, jnp.zeros((LANES - SUB, rows), jnp.float32)], axis=0)
    return jnp.transpose(full)


def lane_of(columns, index):
    return jnp.sum(jnp.where(iota(columns.shape, 1) == index, columns, 0.0), axis=1, keepdims=True)


def back_kernel(groups, local_count, *refs):
    grds, (down, back, grd) = refs[:-3], refs[-3:]
    _, first_local = place_of(groups, local_count)
    piece_rows = grd.shape[0] // len(grds)
    for n, piece in enumerate(grds):
        grd[pl.ds(n * piece_rows, piece_rows), :] = piece[...]
    g = grd[...]
    for i in range(back.shape[0]):
        for j in range(back.shape[2] // STEP):
            cols = pl.ds(j * STEP, STEP)
            back[i, :, cols] = jnp.dot(g, down[first_local + i, :, cols], preferred_element_type=jnp.float32)


def first_kernel(groups, local_count, count, width, kept, *refs):
    toks, (backs, gate_t, gate_up, hid, dpre, grads, tok) = refs[:count], refs[count:]
    _, first_local = place_of(groups, local_count)
    rows = tok.shape[0]
    piece_rows = rows // count
    hidden_units = hid.shape[2]
    for n in range(count):
        tok[pl.ds(n * piece_rows, piece_rows), :] = toks[n][:, :width]
    gates = to_columns(gate_t[...], rows) * kept
    lane = iota((rows, LANES), 1)
    t = tok[...]
    gate_grads = jnp.zeros((rows, LANES), jnp.float32)
    for i in range(hid.shape[0]):
        e = first_local + i
        weight = lane_of(gates, e)
        total = jnp.zeros((rows, 1), jnp.float32)
        for j in range(hidden_units // STEP):
            cols = pl.ds(j * STEP, STEP)
            ups = pl.ds(hidden_units + j * STEP, STEP)
            a = jnp.dot(t, gate_up[e, :, cols], preferred_element_type=jnp.float32)
            b = jnp.dot(t, gate_up[e, :, ups], preferred_element_type=jnp.float32)
            back = backs[i, :, cols]
            s = jax.nn.sigmoid(a)
            swish = a * s
            hidden = swish * b
            total = total + jnp.sum(hidden * back, axis=1, keepdims=True)
            back = back * weight
            hid[i, :, cols] = (hidden * weight).astype(jnp.bfloat16)
            dpre[i, :, cols] = (back * b * s * (1.0 + a * (1.0 - s))).astype(jnp.bfloat16)
            dpre[i, :, ups] = (back * swish).astype(jnp.bfloat16)
        gate_grads = jnp.where(lane == e, total, gate_grads)
    grads[...] = gate_grads


def kept_columns(groups, local_count, levels, mask_ref, far, spare, named_t, place_t, cap_t):
    far_pairs = []
    for even, odd in levels:
        n = 1 if even == odd else 2
        far_pairs.append(far[:n])
        far = far[n:]
    rows = named_t.shape[1]
    group_rows = rows // groups
    sub = iota((SUB, 1), 0)
    mask = jnp.zeros((SUB, 1), jnp.int32)
    for l in range(local_count):
        mask = jnp.where(sub == l, mask_ref[l], mask)
    group_of = iota((SUB, rows), 1) // group_rows
    limit = jnp.zeros((SUB, rows), jnp.float32)
    for g in range(groups):
        other = jnp.zeros((SUB, 1), jnp.float32)
        if groups == 2:
            other = jnp.where(mask == 1, spare[:, 1 - g : 2 - g], other)
        for (even, odd), refs_at in zip(levels, far_pairs):
            if even == odd:
                other = jnp.where(mask == even, refs_at[0][:, g : g + 1], other)
                continue
            core = lax.axis_index("dp") % 2
            level, crossed = jnp.where(core == 0, even, odd), jnp.where(core == 0, odd, even)
            other = jnp.where(mask == level, refs_at[0][:, g : g + 1], other)
            other = jnp.where(mask == crossed, refs_at[1][:, 1 - g : 2 - g], other)
        limit = jnp.where(group_of == g, cap_t[:, g : g + 1] + jnp.minimum(other, float(OVF)), limit)
    kept = jnp.where((named_t[...] > 0.0) & (place_t[...] < limit), 1.0, 0.0)
    return to_columns(kept, rows)


def second_kernel(groups, local_count, width, kept, hid, dpre, grads, gate_up, down, *outs):
    first_expert, first_local = place_of(groups, local_count)
    group_rows = hid.shape[1] // groups

    def product(left, right, cols):
        total = None
        for i in range(hid.shape[0]):
            part = lax.dot_general(
                right[first_local + i, cols, :], left[i], (((1,), (1,)), ((), ())), preferred_element_type=jnp.float32
            )
            total = part if total is None else total + part
        return jnp.transpose(total).astype(jnp.bfloat16)

    def store(value, to):
        for g in range(groups):
            outs[g][:, to] = value[g * group_rows : (g + 1) * group_rows]

    for j in range(width // WIDE):
        cols = pl.ds(j * WIDE, WIDE)
        store(product(hid, down, cols), cols)
        store(product(dpre, gate_up, cols), pl.ds(width + j * WIDE, WIDE))
    value = jnp.where(kept > 0.0, grads[...], 0.0)
    high = value.astype(jnp.bfloat16).astype(jnp.float32)
    high_at = pltpu.roll(high, first_expert, 1)
    low_at = pltpu.roll(value - high, first_expert + EXPERTS, 1)
    table = high_at + low_at
    store(table.astype(jnp.bfloat16), pl.ds(2 * width, LANES))


def experts_kernel(groups, local_count, count, width, levels, mask_ref, *refs):
    n = sum(1 if even == odd else 2 for even, odd in levels)
    far, refs = refs[:n], refs[n:]
    (spare, named_t, place_t, cap_t, gate_t), refs = refs[:5], refs[5:]
    toks, backs, refs = refs[:count], refs[count], refs[count + 1 :]
    (gate_up, down), refs = refs[:2], refs[2:]
    outs, (tok, hid, dpre, grads) = refs[:groups], refs[groups:]
    kept = kept_columns(groups, local_count, levels, mask_ref, far, spare, named_t, place_t, cap_t)
    first_kernel(groups, local_count, count, width, kept, *toks, backs, gate_t, gate_up, hid, dpre, grads, tok)
    second_kernel(groups, local_count, width, kept, hid, dpre, grads, gate_up, down, *outs)


def join_kernel(own, other, *outs):
    rows = outs[0].shape[0]
    for n, out in enumerate(outs):
        at = slice(n * rows, (n + 1) * rows)
        out[...] = (own[at, :].astype(jnp.float32) + other[at, :].astype(jnp.float32)).astype(out.dtype)


def finish_kernel(width, *refs):
    parts, (routes_t, layer_out, input_grad, gate_grad_t) = refs[:-4], refs[-4:]

    def total(cols):
        out = parts[0][:, cols].astype(jnp.float32)
        for part in parts[1:]:
            out = out + part[:, cols].astype(jnp.float32)
        return out

    layer_out[...] = total(slice(0, width)).astype(jnp.bfloat16)
    input_grad[...] = total(slice(width, 2 * width)).astype(jnp.bfloat16)
    table = total(slice(2 * width, 2 * width + LANES))
    tok_count = table.shape[0]
    table = jnp.concatenate([table, jnp.zeros((LANES - tok_count, LANES), jnp.float32)], axis=0)
    by_expert = jnp.transpose(table)[:, :tok_count]
    ids = routes_t[...]
    out = jnp.zeros(ids.shape, jnp.float32)
    for e in range(EXPERTS):
        value = by_expert[e : e + 1, :] + by_expert[EXPERTS + e : EXPERTS + e + 1, :]
        out = jnp.where(ids == e, value, out)
    gate_grad_t[...] = out


def kernel(body, out_shape, in_specs, scratch=(), limit=4, flops=0):
    vm = pl.BlockSpec(memory_space=VM)
    return pl.pallas_call(
        body,
        out_shape=out_shape,
        in_specs=in_specs,
        out_specs=jax.tree.map(lambda _: vm, out_shape),
        scratch_shapes=scratch,
        compiler_params=pltpu.CompilerParams(vmem_limit_bytes=limit * MIB),
        cost_estimate=pl.CostEstimate(flops=flops, bytes_accessed=0, transcendentals=0) if flops else None,
    )


def body(tokens, grad_out, gate_probs, routes, capacity, pair_mask, gate_up_weight, down_weight):
    tok_count, width = tokens.shape
    local_count, _, hidden_units = down_weight.shape
    group_size = lax.axis_size("expert")
    replicas = lax.axis_size("dp")
    groups = 2 if local_count % 2 == 0 and replicas % 2 == 0 else 1
    per_device = local_count // groups
    bf16, f32 = jnp.bfloat16, jnp.float32
    vm, sm = pl.BlockSpec(memory_space=VM), pl.BlockSpec(memory_space=pltpu.SMEM)
    hbm = pl.BlockSpec(memory_space=pltpu.HBM)
    array = jax.ShapeDtypeStruct
    routes_t = routes.T
    gate_up = pltpu.with_memory_space_constraint(gate_up_weight, VM)
    down = pltpu.with_memory_space_constraint(down_weight, VM)

    packed = kernel(
        prep_kernel,
        array((tok_count, width + LANES), bf16),
        [hbm] * 3 + [sm if local_count == 1 else hbm],
        [
            VM((TOPK, tok_count), jnp.int32),
            VM((TOPK, tok_count), bf16),
            pltpu.SMEM((1, local_count), jnp.int32),
            VM((tok_count, LANES), f32),
            pltpu.SemaphoreType.DMA((4,)),
        ],
        flops=LURE,
    )(
        *(pltpu.with_memory_space_constraint(v, pltpu.HBM) for v in (tokens, routes_t, gate_probs.T)),
        capacity if local_count == 1 else pltpu.with_memory_space_constraint(capacity, pltpu.HBM),
    )

    def gathered(piece):
        pieces = [piece] + [swapped(piece, "expert", k) for k in range(1, group_size)]
        if groups == 2:
            pieces += [swapped(p, "dp", 1) for p in pieces]
        return pieces

    toks = gathered(packed)
    grds = gathered(grad_out)
    count = len(toks)
    rows = count * tok_count
    total_width = 2 * width + LANES

    side_spec = pl.BlockSpec((tok_count, LANES), lambda i: (0, width // LANES))
    small, wide = array((SUB, LANES), f32), array((SUB, rows), f32)
    spare, named_t, place_t, gate_t, cap_t = pl.pallas_call(
        functools.partial(tables_kernel, group_size, groups, local_count, tok_count),
        out_shape=[small, wide, wide, wide, small],
        grid=(1,),
        in_specs=[side_spec] * count,
        out_specs=[pl.BlockSpec((SUB, s.shape[1]), lambda i: (0, 0)) for s in (small, wide, wide, wide, small)],
        compiler_params=pltpu.CompilerParams(vmem_limit_bytes=4 * MIB),
        name="tables",
    )(*toks)
    group_rows = rows // groups
    masks = [1 << b for b in range(groups - 1, replicas.bit_length() - 1)]
    if groups == 2:
        levels = tuple(zip(masks[::2], masks[1::2])) + ((masks[-1],) * 2,) * (len(masks) % 2)
    else:
        levels = tuple(zip(masks, masks))
    far = []
    for even, odd in levels:
        far.append(swapped_by_core(spare, even, odd))
        if even != odd:
            far.append(swapped(far[-1], "dp", 1))
    backs = kernel(
        functools.partial(back_kernel, groups, local_count),
        array((per_device, rows, hidden_units), f32),
        [vm] * (count + 1),
        [VM((rows, width), bf16)],
    )(*grds, down)
    parts = kernel(
        functools.partial(experts_kernel, groups, local_count, count, width, levels),
        [array((group_rows, total_width), bf16)] * groups,
        [sm] + [vm] * (len(far) + 8 + count),
        [
            VM((rows, width), bf16),
            VM((per_device, rows, hidden_units), bf16),
            VM((per_device, rows, 2 * hidden_units), bf16),
            VM((rows, LANES), f32),
        ],
        8,
    )(pair_mask, *far, spare, named_t, place_t, cap_t, gate_t, *toks, backs, gate_up, down)
    block = array((tok_count, total_width), bf16)
    if groups == 2:
        other = swapped(parts[1], "dp", 1)
        blocks = kernel(join_kernel, [block] * group_size, [vm, vm])(parts[0], other)
    else:
        blocks = [parts[0][k * tok_count : (k + 1) * tok_count] for k in range(group_size)]
    mine = [blocks[0]] + [swapped(blocks[k], "expert", k) for k in range(1, group_size)]
    layer_out, input_grad, gate_grad_t = kernel(
        functools.partial(finish_kernel, width),
        [array((tok_count, width), bf16), array((tok_count, width), bf16), array((TOPK, tok_count), f32)],
        [vm] * (group_size + 1),
    )(*mine, routes_t)
    return layer_out, input_grad, gate_grad_t.T


def solution(mesh):
    return jax.shard_map(
        body,
        mesh=mesh,
        in_specs=(
            P(("dp", "expert"), None),
            P(("dp", "expert"), None),
            P(("dp", "expert"), None),
            P(("dp", "expert"), None),
            P("dp", "expert"),
            P("expert"),
            P("expert", None, None),
            P("expert", None, None),
        ),
        out_specs=(P(("dp", "expert"), None), P(("dp", "expert"), None), P(("dp", "expert"), None)),
        check_vma=False,
    )
```
